256 devices in a mesh: gx: 32 (over z, x), st: 8 (over y, core).
Axes of the slice: x: 4, y: 4, z: 8, core: 2. Of those that a mesh axis runs over, the one named last changes fastest.
Arguments:
- checkpoint: float32 [26, 256, 64, 128], P(None, ('gx', 'st')), may hold values from -0.5 to 1, as said below
- adjoint_in: float32 [26, 256, 64, 128], P(None, 'gx', 'st'), may hold values from -6 to 6
- solid_mask: int32 [256, 64, 128], P('gx', 'st'), may hold values 0 or 1
- tile_map: int32 [256, 64], P('gx', 'st'), may hold values from 0 to 4095
- theta: float32 [4096], replicated, may hold values from 0.8 to 1.2
- first_moment: float32 [4096], replicated, may hold values from -6 to 6
- second_moment: float32 [4096], replicated, may hold values from 1 to 30
Outputs:
- adjoint_out: float32 [26, 256, 64, 128], P(None, 'gx', 'st')
- theta_new: float32 [4096], replicated
- first_new: float32 [4096], replicated
- second_new: float32 [4096], replicated
- nusselt: float32 [], replicated
The draws below stay inside these ranges and needn't reach their ends.
Inputs may be any that keep to these rules, and one draw needn't show every extreme that they name: `checkpoint`: populations near a local equilibrium; the flow populations of a cell sum to a density near 1.
All inputs are finite; a program needn't handle non-finite values. No bound on the sum of `solid_mask` on one device may be relied on, other than what follows from the above.
Results may differ from the reference program's by a relative error of at most 0.0001.
Values sent between devices are 32-bit elements; how exact they have to be, the bound alone decides.
No kernel may reach another device: no remote copies, remote signals or barrier semaphores. Data moves between devices by JAX's collectives and lax.ppermute only.
A program may use at most 64 MiB of HBM per device.

```python
import math
import jax
import jax.numpy as jnp
import numpy as np
from jax import lax

NZ = 128
STEPS = 4
NTILE = 4096
ADAM_STEP = 100
NX = 256
NY = 64


VELOCITY = np.array([[0, 0, 0], [1, 0, 0], [-1, 0, 0], [0, 1, 0], [0, -1, 0], [0, 0, 1], [0, 0, -1], [1, 1, 0], [-1, -1, 0], [1, -1, 0], [-1, 1, 0], [1, 0, 1], [-1, 0, -1], [1, 0, -1], [-1, 0, 1], [0, 1, 1], [0, -1, -1], [0, 1, -1], [0, -1, 1], [0, 0, 0], [1, 0, 0], [-1, 0, 0], [0, 1, 0], [0, -1, 0], [0, 0, 1], [0, 0, -1]], dtype=np.int32)


WEIGHTS = np.array([1.0 / 3.0] + [1.0 / 18.0] * 6 + [1.0 / 36.0] * 12 + [0.25] + [0.125] * 6, dtype=np.float32)


def column_drawn(values):
    return jnp.asarray(values, jnp.float32).reshape(-1, 1, 1, 1)


def rough_noise(subkey, shape):
    return jax.random.truncated_normal(subkey, -3.0, 3.0, shape, jnp.float32)


def draw_checkpoint(key, part):
    keys = jax.random.split(key, 7)
    shape_cells = (NX, NY, NZ)
    position = jnp.arange(NX, dtype=jnp.float32) / max(NX - 1, 1)
    growth = 1.0 + 2.0 * position
    growth = growth[:, None, None]
    density = 1.0 + 0.02 * rough_noise(keys[0], shape_cells)
    speed_x = 0.03 * growth * rough_noise(keys[1], shape_cells)
    speed_y = 0.03 * growth * rough_noise(keys[2], shape_cells)
    base_z = rough_noise(keys[3], shape_cells)
    speed_z = 0.03 * growth * base_z
    temper = 0.5 + 0.03 * growth * (0.6 * base_z + 0.8 * rough_noise(keys[4], shape_cells))
    projected = column_drawn(VELOCITY[:19, 0]) * speed_x + column_drawn(VELOCITY[:19, 1]) * speed_y + column_drawn(VELOCITY[:19, 2]) * speed_z
    square_speed = speed_x * speed_x + speed_y * speed_y + speed_z * speed_z
    flow_part = column_drawn(WEIGHTS[:19]) * (density + 3.0 * projected + 4.5 * projected * projected - 1.5 * square_speed)
    flow_part = flow_part + column_drawn(WEIGHTS[:19]) * 0.02 * rough_noise(keys[5], (19,) + shape_cells)
    heat_proj = column_drawn(VELOCITY[19:, 0]) * speed_x + column_drawn(VELOCITY[19:, 1]) * speed_y + column_drawn(VELOCITY[19:, 2]) * speed_z
    heat_part = column_drawn(WEIGHTS[19:]) * temper * (1.0 + 4.0 * heat_proj)
    heat_part = heat_part + column_drawn(WEIGHTS[19:]) * 0.02 * rough_noise(keys[6], (7,) + shape_cells)
    return jnp.concatenate([flow_part, heat_part], 0).astype(jnp.float32)


def plant(values, stream_key, least, largest):
    shape = values.shape
    place = [jax.random.randint(jax.random.fold_in(stream_key, axis), (), 0, shape[axis]) for axis in range(len(shape))]
    values = values.at[tuple(place)].set(least)
    longest = shape.index(max(shape))
    place[longest] = (place[longest] + 1) % shape[longest]
    return values.at[tuple(place)].set(largest)


def level_of(key, extent, cuts, smallest, largest):
    gain = 1.0
    for dim, blocks in cuts:
        heights = jax.random.uniform(jax.random.fold_in(jax.random.fold_in(key, 6), dim), (blocks,), jnp.float32, smallest / len(cuts), largest / len(cuts))
        gain = gain * jnp.repeat(jnp.exp(heights), extent[dim] // blocks).reshape((-1,) + (1,) * (len(extent) - 1 - dim))
    return gain


def bell_draw(stream_key, dims, width, limit, shards=(), kind=jnp.bfloat16):
    values = width * jax.random.normal(stream_key, dims, jnp.float32)
    if shards:
        values = values * level_of(stream_key, dims, shards, -0.22, 0.18)
    return jnp.clip(values, -limit, limit).astype(kind)


def setup_inputs(seed: int = 0) -> dict:
    seeds = jax.random.split(jax.random.key(seed), 8)
    checkpoint = draw_checkpoint(jax.random.fold_in(seeds[7], 71), 0)
    adjoint_in = bell_draw(seeds[1], (26, NX, NY, NZ), 1.0, 6.0, ((1, 32), (2, 8)), jnp.float32)
    solid_mask = plant((jax.random.randint(seeds[2], (NX, NY, NZ), 0, 8) < 1).astype(jnp.int32), jax.random.fold_in(seeds[2], 1), 0, 1)
    tile_map = plant(jax.random.randint(seeds[3], (NX, NY), 0, NTILE), jax.random.fold_in(seeds[3], 1), 0, NTILE - 1).astype(jnp.int32)
    theta = jnp.clip(jax.random.uniform(seeds[4], (NTILE,), jnp.float32, 0.8, 1.2), 0.8, 1.2)
    first_moment = bell_draw(seeds[5], (NTILE,), 1.0, 6.0, (), jnp.float32)
    second_moment = jnp.clip(jnp.exp(jax.random.uniform(seeds[6], (NTILE,), jnp.float32, math.log(1.0), math.log(30.0))), 1.0, 30.0)
    return dict(checkpoint=checkpoint, adjoint_in=adjoint_in, solid_mask=solid_mask, tile_map=tile_map, theta=theta, first_moment=first_moment, second_moment=second_moment)


VELOCITY = np.array([[0, 0, 0], [1, 0, 0], [-1, 0, 0], [0, 1, 0], [0, -1, 0], [0, 0, 1], [0, 0, -1], [1, 1, 0], [-1, -1, 0], [1, -1, 0], [-1, 1, 0], [1, 0, 1], [-1, 0, -1], [1, 0, -1], [-1, 0, 1], [0, 1, 1], [0, -1, -1], [0, 1, -1], [0, -1, 1], [0, 0, 0], [1, 0, 0], [-1, 0, 0], [0, 1, 0], [0, -1, 0], [0, 0, 1], [0, 0, -1]], dtype=np.int32)
WEIGHTS = np.array([1.0 / 3.0] + [1.0 / 18.0] * 6 + [1.0 / 36.0] * 12 + [0.25] + [0.125] * 6, dtype=np.float32)
OPPOSITE = np.array([0, 2, 1, 4, 3, 6, 5, 8, 7, 10, 9, 12, 11, 14, 13, 16, 15, 18, 17, 19, 21, 20, 23, 22, 25, 24], dtype=np.int32)
TAU_FLOW = 0.8
TAU_HEAT = 0.8
BUOYANCY = 0.001
MEAN_TEMP = 0.5
KAPPA = 0.075
rising_heat = 24
LEARN_RATE = 0.05
BETA_ONE = 0.9
BETA_TWO = 0.99
ADAM_EPS = 1e-08

def column(values):
    return jnp.asarray(values, jnp.float32).reshape(-1, 1, 1, 1)

def collide(populations):
    flow_part = populations[:19]
    heat_part = populations[19:]
    density = lax.optimization_barrier(jnp.sum(flow_part, 0))
    speed_x = lax.optimization_barrier(jnp.sum(flow_part * column(VELOCITY[:19, 0]), 0))
    speed_y = lax.optimization_barrier(jnp.sum(flow_part * column(VELOCITY[:19, 1]), 0))
    speed_z = lax.optimization_barrier(jnp.sum(flow_part * column(VELOCITY[:19, 2]), 0))
    temper = lax.optimization_barrier(jnp.sum(heat_part, 0))
    forced_z = speed_z + TAU_FLOW * BUOYANCY * (temper - MEAN_TEMP)
    projected = column(VELOCITY[:19, 0]) * speed_x + column(VELOCITY[:19, 1]) * speed_y + column(VELOCITY[:19, 2]) * forced_z
    square_speed = speed_x * speed_x + speed_y * speed_y + forced_z * forced_z
    equilibrium = column(WEIGHTS[:19]) * (density + 3.0 * projected + 4.5 * projected * projected - 1.5 * square_speed)
    flow_post = flow_part - (flow_part - equilibrium) / TAU_FLOW
    heat_proj = column(VELOCITY[19:, 0]) * speed_x + column(VELOCITY[19:, 1]) * speed_y + column(VELOCITY[19:, 2]) * speed_z
    heat_equil = column(WEIGHTS[19:]) * temper * (1.0 + 4.0 * heat_proj)
    heat_post = heat_part - (heat_part - heat_equil) / TAU_HEAT
    return jnp.concatenate([flow_post, heat_post], 0)

def shift_depth(field, step_z):
    if step_z == 1:
        return jnp.concatenate([jnp.zeros_like(field[..., :1]), field[..., :-1]], -1)
    if step_z == -1:
        return jnp.concatenate([field[..., 1:], jnp.zeros_like(field[..., :1])], -1)
    return field

def bounce_table(solid_mask):
    solid_cells = solid_mask.astype(jnp.float32)
    padded = jnp.pad(solid_cells, ((0, 0), (0, 0), (1, 1)), constant_values=1.0)
    wall_layer = jnp.pad(jnp.zeros_like(solid_cells), ((0, 0), (0, 0), (1, 1)), constant_values=1.0)
    depth_cells = solid_cells.shape[2]
    sources = []
    for component in range(26):
        step_x = int(VELOCITY[component, 0])
        step_y = int(VELOCITY[component, 1])
        step_z = int(VELOCITY[component, 2])
        source = jnp.roll(padded, (step_x, step_y), axis=(0, 1))[:, :, 1 - step_z:1 - step_z + depth_cells]
        if component >= 19:
            source = source - 2.0 * wall_layer[:, :, 1 - step_z:1 - step_z + depth_cells]
        sources.append(source)
    return jnp.stack(sources)

def pull_all(field, velocity):
    pieces = []
    for component in range(26):
        step_x = int(velocity[component, 0])
        step_y = int(velocity[component, 1])
        step_z = int(velocity[component, 2])
        shifted = jnp.roll(field[component], (step_x, step_y), axis=(0, 1))
        pieces.append(shift_depth(shifted, step_z))
    return jnp.stack(pieces)

def propagate(collided, bounce, plate_temp):
    kept_share = 1.0 - jnp.abs(bounce)
    result = kept_share * pull_all(collided, VELOCITY) + bounce * collided[OPPOSITE]
    return result.at[rising_heat, :, :, 0].add(0.25 * plate_temp)

def propagate_adjoint(adjoint, bounce):
    kept_share = 1.0 - jnp.abs(bounce)
    return pull_all(kept_share * adjoint, -VELOCITY) + (bounce * adjoint)[OPPOSITE]

def flux_seed(populations, fluid):
    speed_z = lax.optimization_barrier(jnp.sum(populations[:19] * column(VELOCITY[:19, 2]), 0))
    temper = lax.optimization_barrier(jnp.sum(populations[19:], 0))
    flow_seed = fluid * column(VELOCITY[:19, 2]) * temper
    heat_seed = jnp.broadcast_to(fluid * speed_z, (7,) + speed_z.shape)
    return (speed_z, temper, jnp.concatenate([flow_seed, heat_seed], 0))

def adam_update(theta, first_moment, second_moment, tile_grad):
    first_new = BETA_ONE * first_moment + (1.0 - BETA_ONE) * tile_grad
    second_new = BETA_TWO * second_moment + (1.0 - BETA_TWO) * tile_grad * tile_grad
    first_hat = first_new / (1.0 - BETA_ONE ** ADAM_STEP)
    second_hat = second_new / (1.0 - BETA_TWO ** ADAM_STEP)
    theta_new = theta - LEARN_RATE * first_hat / (jnp.sqrt(second_hat) + ADAM_EPS)
    return (theta_new, first_new, second_new)

def reference(checkpoint, adjoint_in, solid_mask, tile_map, theta, first_moment, second_moment):
    bounce = bounce_table(solid_mask)
    plate_temp = theta[tile_map]
    fluid = 1.0 - solid_mask.astype(jnp.float32)
    current = checkpoint
    stored = []
    for counter in range(STEPS):
        stored.append(current)
        current = propagate(collide(current), bounce, plate_temp)
    speed_z, temper, seed_field = flux_seed(current, fluid)
    heat_sum = jnp.sum(fluid * speed_z * temper)
    nusselt = 1.0 + heat_sum / (KAPPA * solid_mask.shape[0] * solid_mask.shape[1])
    adjoint = adjoint_in + (nusselt - 1.0) * seed_field
    plate_grad = jnp.zeros(plate_temp.shape, jnp.float32)
    for counter in range(STEPS - 1, -1, -1):
        plate_grad = plate_grad + 0.25 * adjoint[rising_heat, :, :, 0]
        spread = propagate_adjoint(adjoint, bounce)
        adjoint = jax.vjp(collide, stored[counter])[1](spread)[0]
    tile_grad = jax.ops.segment_sum(plate_grad.reshape(-1), tile_map.reshape(-1), num_segments=NTILE)
    theta_new, first_new, second_new = adam_update(theta, first_moment, second_moment, tile_grad)
    return (adjoint, theta_new, first_new, second_new, nusselt)
```

```python
import functools

import jax
import jax.numpy as jnp
import numpy as np
from jax import lax
from jax.experimental import pallas as pl
from jax.experimental.pallas import tpu as pltpu
from jax.sharding import PartitionSpec as P

ADAM_STEP = 100

VELOCITY = np.array(
    [
        [0, 0, 0],
        [1, 0, 0],
        [-1, 0, 0],
        [0, 1, 0],
        [0, -1, 0],
        [0, 0, 1],
        [0, 0, -1],
        [1, 1, 0],
        [-1, -1, 0],
        [1, -1, 0],
        [-1, 1, 0],
        [1, 0, 1],
        [-1, 0, -1],
        [1, 0, -1],
        [-1, 0, 1],
        [0, 1, 1],
        [0, -1, -1],
        [0, 1, -1],
        [0, -1, 1],
        [0, 0, 0],
        [1, 0, 0],
        [-1, 0, 0],
        [0, 1, 0],
        [0, -1, 0],
        [0, 0, 1],
        [0, 0, -1],
    ],
    dtype=np.int32,
)
VEL = [tuple(int(v) for v in row) for row in VELOCITY]
OPP = [0, 2, 1, 4, 3, 6, 5, 8, 7, 10, 9, 12, 11, 14, 13, 16, 15, 18, 17, 19, 21, 20, 23, 22, 25, 24]
FLOW_PAIRS = [(i, i + 1) for i in range(1, 19, 2)]
HEAT_PAIRS = [(20, 21), (22, 23), (24, 25)]
INV_TAU = 1.25
KEEP = 1.0 - INV_TAU
LIFT = 0.8 * 0.001
MEAN_TEMP = 0.5
KAPPA = 0.075
RISING = 24
LEARN_RATE = 0.05
BETA_ONE = 0.9
BETA_TWO = 0.99
ADAM_EPS = 1e-08

HALO = 4
OWN = 8
WIDE = OWN + 2 * HALO
DEPTH = 128
INTERPRET = False


def weight(i):
    if i < 19:
        return 1.0 / 3.0 if i == 0 else (1.0 / 18.0 if i < 7 else 1.0 / 36.0)
    return 0.25 if i == 19 else 0.125


def call(kernel, outs, scratch=(), cost=0):
    return pl.pallas_call(
        kernel,
        out_shape=[jax.ShapeDtypeStruct(s, jnp.float32) for s in outs],
        scratch_shapes=list(scratch),
        compiler_params=pltpu.CompilerParams(vmem_limit_bytes=56 << 20),
        cost_estimate=pl.CostEstimate(flops=cost, bytes_accessed=1 << 20, transcendentals=0),
        interpret=INTERPRET,
    )


class At:
    def __init__(self, index, offset):
        self.index, self.offset = index, offset

    def by(self, more):
        return self.index + (self.offset + more) if self.offset + more else self.index


def loop(count, fn):
    lax.fori_loop(0, count, lambda i, c: (fn(i), c)[1], 0)


def shifted(value, step_y, step_z):
    if step_y:
        value = pltpu.roll(value, step_y % value.shape[0], 0)
    if step_z:
        value = pltpu.roll(value, step_z % DEPTH, 1)
    return value


def lane_is(k, rows=WIDE):
    return lax.broadcasted_iota(jnp.int32, (rows, DEPTH), 1) == k


def table_of(i):
    if i >= 24:
        return i - 6
    if i >= 19:
        return i - 20
    return i - 1


def add_all(values):
    total = values[0]
    for value in values[1:]:
        total = total + value
    return total


def signed_sum(terms):
    total = None
    for sign, value in terms:
        if total is None:
            total = value if sign > 0 else -value
        else:
            total = total + value if sign > 0 else total - value
    return total


def moments(s):
    diff = {}
    parts = [s[0]]
    for i, j in FLOW_PAIRS:
        parts.append(s[i] + s[j])
        diff[i] = s[i] - s[j]
    density = add_all(parts)
    speed = []
    for axis in range(3):
        speed.append(signed_sum([(VEL[i][axis], diff[i]) for i, _ in FLOW_PAIRS if VEL[i][axis]]))
    temper = add_all([s[i] for i in range(19, 26)])
    return density, speed, temper


def collided(s, density, speed, temper):
    ux, uy, uz = speed
    vz = uz + LIFT * (temper - MEAN_TEMP)
    vel = (ux, uy, vz)
    base = density - 1.5 * (ux * ux + uy * uy + vz * vz)
    out = [None] * 26
    out[0] = KEEP * s[0] + (INV_TAU * weight(0)) * base
    for i, j in FLOW_PAIRS:
        proj = signed_sum([(VEL[i][a], vel[a]) for a in range(3) if VEL[i][a]])
        factor = INV_TAU * weight(i)
        even = factor * base + (4.5 * factor) * (proj * proj)
        odd = (3.0 * factor) * proj
        out[i] = KEEP * s[i] + (even + odd)
        out[j] = KEEP * s[j] + (even - odd)
    out[19] = KEEP * s[19] + (INV_TAU * weight(19)) * temper
    scaled = (INV_TAU * weight(20)) * temper
    for (i, j), u in zip(HEAT_PAIRS, (ux, uy, uz)):
        odd = scaled * (4.0 * u)
        out[i] = KEEP * s[i] + (scaled + odd)
        out[j] = KEEP * s[j] + (scaled - odd)
    return out


def pack_kernel(plane, out):
    def one(c):
        for slot in range(8):
            if slot == 0:
                out[slot, c, 0:4] = plane[c, 60:64]
                out[slot, c, 4:16] = plane[c, 0:12]
            elif slot == 7:
                out[slot, c, 0:12] = plane[c, 52:64]
                out[slot, c, 12:16] = plane[c, 0:4]
            else:
                out[slot, c] = plane[c, 8 * slot - 4 : 8 * slot + 12]

    loop(26, one)


def table_kernel(region, table):
    first = lane_is(0)
    last = lane_is(DEPTH - 1)

    def one(n):
        at = At(n, 1)
        x = at.by(0)
        for i in range(1, 19):
            cx, cy, cz = VEL[i]
            value = shifted(region[0, at.by(-cx)], cy, cz)
            if cz:
                edge = first if cz > 0 else last
                if i in (5, 6):
                    table[x, table_of(i + 19)] = jnp.where(edge, -1.0, value)
                value = jnp.where(edge, 1.0, value)
            table[x, table_of(i)] = value

    loop(WIDE - 2, one)


def streamed(p, table, at):
    x = at.by(0)
    s = []
    for i in range(26):
        if i in (0, 19):
            s.append(p[x, i])
            continue
        cx, cy, cz = VEL[i]
        moved = shifted(p[at.by(-cx), i], cy, cz)
        t = table[x, table_of(i)]
        back = p[x, OPP[i]]
        if i >= 24:
            back = t * back
        s.append(jnp.where(t == 0.0, moved, back))
    return s


def forward_kernel(left, own, right, table, region, mom, edge, edge_lo, edge_hi, heat, pa, pb, mom3):
    first = lane_is(0)

    def start(src, off):
        def one(x):
            s = [src[x, i] for i in range(26)]
            density, speed, temper = moments(s)
            for a in range(3):
                mom[0, x + off, a] = speed[a]
            mom[0, x + off, 3] = temper
            for i, value in enumerate(collided(s, density, speed, temper)):
                pa[x + off, i] = value

        return one

    loop(HALO, start(left, 0))
    loop(OWN, start(own, HALO))
    loop(HALO, start(right, HALO + OWN))

    def arrive(p, at):
        s = streamed(p, table, at)
        s[RISING] = s[RISING] + jnp.where(first, 0.25 * region[1, at.by(0)], 0.0)
        return s

    src, dst = pa, pb
    for k in range(1, 4):

        def one(n, k=k, src=src, dst=dst):
            at = At(n, k)
            x = at.by(0)
            s = arrive(src, at)
            density, speed, temper = moments(s)
            for a, value in enumerate((*speed, temper)):
                if k < 3:
                    mom[k, x, a] = value
                else:
                    mom3[x, a] = value
            for i, value in enumerate(collided(s, density, speed, temper)):
                dst[x, i] = value

        loop(WIDE - 2 * k, one)
        src, dst = dst, src

    heat[...] = jnp.zeros_like(heat)

    def last(n):
        at = At(n, HALO)
        x = at.by(0)
        s = arrive(src, at)
        _, speed, temper = moments(s)
        values = [mom3[x, a] for a in range(4)] + [speed[2], temper]
        for a, value in enumerate(values):
            edge[n, a] = value[4:12]
            edge_lo[n, a] = value[4:8]
            edge_hi[n, a] = value[8:12]
        flux = (1.0 - region[0, x]) * speed[2] * temper
        heat[...] += flux[4:12]

    loop(OWN, last)


def adjoint_cell(lam, table, at, fluids, vel, temper):
    x = at.by(0)
    fluid, fluid_up, fluid_down = fluids
    ux, uy, uz = vel
    vz = uz + LIFT * (temper - MEAN_TEMP)
    v = (ux, uy, vz)

    def mu_of(j):
        cx, cy, cz = VEL[j]
        if j in (0, 19):
            return lam[x, j]
        moved = shifted(lam[at.by(cx), j], -cy, -cz)
        keep = fluid if cz == 0 else (fluid_up if cz > 0 else fluid_down)
        return keep * moved + table[x, table_of(OPP[j])] * lam[x, OPP[j]]

    mu = [mu_of(j) for j in range(26)]
    axis_sum = add_all([mu[i] + mu[j] for i, j in FLOW_PAIRS[:3]])
    pair_sum = {i: mu[i] + mu[j] for i, j in FLOW_PAIRS}
    pair_diff = {i: mu[i] - mu[j] for i, j in FLOW_PAIRS}
    wa, wd = weight(1), weight(7)
    diag = add_all([pair_sum[i] for i, _ in FLOW_PAIRS[3:]])
    zeroth = weight(0) * mu[0] + wa * axis_sum + wd * diag

    def first(a):
        axis = 1 + 2 * a
        rest = signed_sum([(VEL[i][a], pair_diff[i]) for i, _ in FLOW_PAIRS[3:] if VEL[i][a]])
        return wa * pair_diff[axis] + wd * rest

    def second(a, b):
        if a == b:
            rest = add_all([pair_sum[i] for i, _ in FLOW_PAIRS[3:] if VEL[i][a]])
            return wa * pair_sum[1 + 2 * a] + wd * rest
        return wd * signed_sum(
            [(VEL[i][a] * VEL[i][b], pair_sum[i]) for i, _ in FLOW_PAIRS[3:] if VEL[i][a] * VEL[i][b]]
        )

    m2 = {(a, b): second(a, b) for a in range(3) for b in range(a, 3)}
    force = []
    for a in range(3):
        bent = add_all([m2[min(a, b), max(a, b)] * v[b] for b in range(3)])
        force.append(3.0 * first(a) + 9.0 * bent - 3.0 * (v[a] * zeroth))
    heat_diff = [mu[i] - mu[j] for i, j in HEAT_PAIRS]
    heat_even = weight(19) * mu[19] + weight(20) * add_all([mu[i] + mu[j] for i, j in HEAT_PAIRS])
    wh = 4.0 * weight(20)
    heat_odd = add_all([heat_diff[a] * (wh * u) for a, u in enumerate((ux, uy, uz))])
    to_heat = INV_TAU * (LIFT * force[2] + heat_even + heat_odd)
    scaled = wh * temper
    pull = [INV_TAU * (force[a] + scaled * heat_diff[a]) for a in range(3)]
    base = INV_TAU * zeroth
    out = [None] * 26
    out[0] = KEEP * mu[0] + base
    for i, j in FLOW_PAIRS:
        proj = signed_sum([(VEL[i][a], pull[a]) for a in range(3) if VEL[i][a]])
        out[i] = KEEP * mu[i] + (base + proj)
        out[j] = KEEP * mu[j] + (base - proj)
    for i in range(19, 26):
        out[i] = KEEP * mu[i] + to_heat
    return out


def backward_kernel(
    own, gl, gr, slo, shi, ey, el, er, mom, table, region, out_a, out_b, grads, la0, la1, lb0, lb1, late
):
    first = lane_is(0)
    last = lane_is(DEPTH - 1)

    def gather(src, count, off):
        def one(x):
            for i in range(26):
                la0[x + off, i, 0:4] = slo[i, x + off]
                la0[x + off, i, 4:12] = src[i, x]
                la0[x + off, i, 12:16] = shi[i, x + off]

        loop(count, one)

    gather(gl, HALO, 0)
    gather(own, OWN, HALO)
    gather(gr, HALO, HALO + OWN)

    def seed(src, count, off):
        def one(x):
            for a in range(6):
                late[x + off, a] = src[x, a]
            fluid = 1.0 - region[0, x + off]
            up = fluid * src[x, 5]
            zero = jnp.zeros_like(up)
            heat = fluid * src[x, 4]
            for i in range(26):
                if i >= 19:
                    lb0[x + off, i] = heat
                else:
                    cz = VEL[i][2]
                    lb0[x + off, i] = zero if cz == 0 else (up if cz > 0 else -up)

        loop(count, one)

    seed(el, HALO, 0)
    seed(ey, OWN, HALO)
    seed(er, HALO, HALO + OWN)

    def collect(chain, lam, fresh):
        def one(n):
            value = lam[n + HALO, RISING][4:12]
            if fresh:
                grads[chain, n] = value
            else:
                grads[chain, n] += value

        loop(OWN, one)

    bufs = [(la0, la1), (lb0, lb1)]
    for k in range(3, -1, -1):
        for chain, (src, _) in enumerate(bufs):
            collect(chain, src, k == 3)

        def one(n, k=k, bufs=tuple(bufs)):
            at = At(n, HALO - k)
            x = at.by(0)
            fluid = 1.0 - region[0, x]
            fluids = (fluid, jnp.where(last, 0.0, fluid), jnp.where(first, 0.0, fluid))
            state = [late[x, a] if k == 3 else mom[k, x, a] for a in range(4)]
            for chain, (src, dst) in enumerate(bufs):
                lam = adjoint_cell(src, table, at, fluids, state[:3], state[3])
                for i in range(26):
                    if k:
                        dst[x, i] = lam[i]
                    else:
                        (out_a, out_b)[chain][i, n] = lam[i][4:12]

        loop(OWN + 2 * k, one)
        bufs = [(dst, src) for src, dst in bufs]


def split3(value):
    high = value.astype(jnp.bfloat16)
    rest = value - high.astype(jnp.float32)
    mid = rest.astype(jnp.bfloat16)
    low = (rest - mid.astype(jnp.float32)).astype(jnp.bfloat16)
    return high, mid, low


def tile_kernel(cells, ids, theta, first, second, theta_new, first_new, second_new):
    rows = cells.shape[0]
    step = 8

    def one(r, total):
        base = pl.multiple_of(r * step, step)
        value = cells[pl.ds(base, step)]
        ident = ids[pl.ds(base, step)]
        pieces = split3(value)
        upper = ident // DEPTH
        lower = ident - upper * DEPTH
        for q in range(step):
            hot = (
                lax.broadcasted_iota(jnp.int32, (32, DEPTH), 0)
                == jnp.broadcast_to(upper[q : q + 1], (32, DEPTH))
            )
            lhs = jnp.concatenate(
                [
                    jnp.where(hot, jnp.broadcast_to(piece[q : q + 1].astype(jnp.float32), (32, DEPTH)), 0.0)
                    for piece in pieces
                ],
                0,
            ).astype(jnp.bfloat16)
            rhs = jnp.where(
                lax.broadcasted_iota(jnp.int32, (DEPTH, DEPTH), 0)
                == jnp.broadcast_to(lower[q : q + 1], (DEPTH, DEPTH)),
                1.0,
                0.0,
            ).astype(jnp.bfloat16)
            total = total + lax.dot_general(
                lhs, rhs, (((1,), (1,)), ((), ())), preferred_element_type=jnp.float32
            )
        return total

    total = lax.fori_loop(0, rows // step, one, jnp.zeros((96, DEPTH), jnp.float32))
    grad = (total[0:32] + total[32:64]) + total[64:96]
    new_first = BETA_ONE * first[...] + (1.0 - BETA_ONE) * grad
    new_second = BETA_TWO * second[...] + (1.0 - BETA_TWO) * grad * grad
    first_hat = new_first / (1.0 - BETA_ONE**ADAM_STEP)
    second_hat = new_second / (1.0 - BETA_TWO**ADAM_STEP)
    theta_new[...] = theta[...] - LEARN_RATE * first_hat / (jnp.sqrt(second_hat) + ADAM_EPS)
    first_new[...] = new_first
    second_new[...] = new_second


def neighbour(value, axis, step):
    count = lax.axis_size(axis)
    return lax.ppermute(value, axis, [(i, (i + step) % count) for i in range(count)])


def body(checkpoint, adjoint_in, solid_mask, tile_map, theta, first_moment, second_moment):
    vmem = pltpu.VMEM
    f32 = jnp.float32
    packed = call(pack_kernel, [(8, 26, WIDE, DEPTH)])(checkpoint[:, 0])[0]
    own = lax.all_to_all(packed, "st", 0, 0, tiled=True)

    plate = jnp.broadcast_to(theta[tile_map][:, :, None], (OWN, OWN, DEPTH))
    flags = jnp.stack([solid_mask.astype(f32), plate])
    low = neighbour(flags[:, :, 4:8], "st", 1)
    high = neighbour(flags[:, :, 0:4], "st", -1)
    flags = jnp.concatenate([low, flags, high], 2)
    low = neighbour(flags[:, 4:8], "gx", 1)
    high = neighbour(flags[:, 0:4], "gx", -1)
    region = jnp.concatenate([low, flags, high], 1)
    table = call(table_kernel, [(WIDE, 20, WIDE, DEPTH)])(region)[0]

    gl = neighbour(adjoint_in[:, 4:8], "gx", 1)
    gr = neighbour(adjoint_in[:, 0:4], "gx", -1)
    tall = jnp.concatenate([gl, adjoint_in, gr], 1)
    slo = neighbour(tall[:, :, 4:8], "st", 1)
    shi = neighbour(tall[:, :, 0:4], "st", -1)

    left = neighbour(own[4:8], "gx", 1)
    right = neighbour(own[0:4], "gx", -1)
    big = (WIDE, 26, WIDE, DEPTH)
    mom, edge, edge_lo, edge_hi, heat = call(
        forward_kernel,
        [(3, WIDE, 4, WIDE, DEPTH), (OWN, 6, OWN, DEPTH), (OWN, 6, 4, DEPTH), (OWN, 6, 4, DEPTH), (OWN, DEPTH)],
        [vmem(big, f32), vmem(big, f32), vmem((WIDE, 4, WIDE, DEPTH), f32)],
    )(left, own, right, table, region)
    elo = neighbour(edge_hi, "st", 1)
    ehi = neighbour(edge_lo, "st", -1)
    ey = jnp.concatenate([elo, edge, ehi], 2)
    el = neighbour(ey[4:8], "gx", 1)
    er = neighbour(ey[0:4], "gx", -1)

    out_a, out_b, grads = call(
        backward_kernel,
        [(26, OWN, OWN, DEPTH), (26, OWN, OWN, DEPTH), (2, OWN, OWN, DEPTH)],
        [vmem(big, f32)] * 4 + [vmem((WIDE, 6, WIDE, DEPTH), f32)],
    )(adjoint_in, gl, gr, slo, shi, ey, el, er, mom, table, region)

    plate_grad = 0.25 * grads[:, :, :, 0].reshape(2, OWN * OWN)
    count = lax.axis_size("gx") * lax.axis_size("st")
    slot = jnp.concatenate(
        [
            plate_grad[0],
            plate_grad[1],
            tile_map.reshape(-1).astype(f32),
            jnp.broadcast_to(jnp.sum(heat), (OWN * OWN,)),
        ]
    )
    told = lax.all_to_all(
        jnp.broadcast_to(slot[None, None], (count, 1, 256)), ("gx", "st"), 0, 0, tiled=True
    ).reshape(count, 256)
    plate_cells = count * OWN * OWN
    nusselt = 1.0 + jnp.sum(told[:, 192]) / (KAPPA * plate_cells)
    share = nusselt - 1.0
    cells = (told[:, 0:64] + share * told[:, 64:128]).reshape(-1, DEPTH)
    ids = told[:, 128:192].astype(jnp.int32).reshape(-1, DEPTH)
    tiles = (theta.shape[0] // DEPTH, DEPTH)
    theta_new, first_new, second_new = call(tile_kernel, [tiles] * 3)(
        cells, ids, theta.reshape(tiles), first_moment.reshape(tiles), second_moment.reshape(tiles)
    )
    adjoint = out_a + share * out_b
    flat = theta.shape
    return (adjoint, theta_new.reshape(flat), first_new.reshape(flat), second_new.reshape(flat), nusselt)


def solution(mesh):
    return jax.shard_map(
        body,
        mesh=mesh,
        in_specs=(
            P(None, ("gx", "st"), None, None),
            P(None, "gx", "st", None),
            P("gx", "st", None),
            P("gx", "st"),
            P(),
            P(),
            P(),
        ),
        out_specs=(P(None, "gx", "st", None), P(), P(), P(), P()),
        check_vma=False,
    )
```

```python
import functools

import jax
import jax.numpy as jnp
import numpy as np
from jax import lax
from jax.experimental import pallas as pl
from jax.experimental.pallas import tpu as pltpu
from jax.sharding import PartitionSpec as P

ADAM_STEP = 100

VELOCITY = np.array(
    [
        [0, 0, 0],
        [1, 0, 0],
        [-1, 0, 0],
        [0, 1, 0],
        [0, -1, 0],
        [0, 0, 1],
        [0, 0, -1],
        [1, 1, 0],
        [-1, -1, 0],
        [1, -1, 0],
        [-1, 1, 0],
        [1, 0, 1],
        [-1, 0, -1],
        [1, 0, -1],
        [-1, 0, 1],
        [0, 1, 1],
        [0, -1, -1],
        [0, 1, -1],
        [0, -1, 1],
        [0, 0, 0],
        [1, 0, 0],
        [-1, 0, 0],
        [0, 1, 0],
        [0, -1, 0],
        [0, 0, 1],
        [0, 0, -1],
    ],
    dtype=np.int32,
)
VEL = [tuple(int(v) for v in row) for row in VELOCITY]
OPP = [0, 2, 1, 4, 3, 6, 5, 8, 7, 10, 9, 12, 11, 14, 13, 16, 15, 18, 17, 19, 21, 20, 23, 22, 25, 24]
FLOW_PAIRS = [(i, i + 1) for i in range(1, 19, 2)]
HEAT_PAIRS = [(20, 21), (22, 23), (24, 25)]
INV_TAU = 1.25
KEEP = 1.0 - INV_TAU
LIFT = 0.8 * 0.001
MEAN_TEMP = 0.5
KAPPA = 0.075
RISING = 24
LEARN_RATE = 0.05
BETA_ONE = 0.9
BETA_TWO = 0.99
ADAM_EPS = 1e-08

HALO = 4
OWN = 8
WIDE = OWN + 2 * HALO
DEPTH = 128
INTERPRET = False


def weight(i):
    if i < 19:
        return 1.0 / 3.0 if i == 0 else (1.0 / 18.0 if i < 7 else 1.0 / 36.0)
    return 0.25 if i == 19 else 0.125


def call(kernel, outs, scratch=(), mib=8, scalars=0, inputs=None, out_specs=None):
    extra = {}
    if scalars:
        extra["in_specs"] = [pl.BlockSpec(memory_space=pltpu.SMEM)] * scalars + [
            pl.BlockSpec(memory_space=pltpu.VMEM)
        ] * (inputs - scalars)
    if out_specs:
        extra["out_specs"] = [pl.BlockSpec(memory_space=space) for space in out_specs]
    return pl.pallas_call(
        kernel,
        out_shape=[jax.ShapeDtypeStruct(s, jnp.float32) for s in outs],
        scratch_shapes=list(scratch),
        compiler_params=pltpu.CompilerParams(vmem_limit_bytes=mib << 20),
        interpret=INTERPRET,
        **extra,
    )


class At:
    def __init__(self, index, offset):
        self.index, self.offset = index, offset

    def by(self, more):
        return self.index + (self.offset + more) if self.offset + more else self.index


def loop(count, fn):
    lax.fori_loop(0, count, lambda i, c: (fn(i), c)[1], 0)


def shifted(value, step_y, step_z):
    if step_y:
        value = pltpu.roll(value, step_y % value.shape[0], 0)
    if step_z:
        value = pltpu.roll(value, step_z % DEPTH, 1)
    return value


def lane_is(k, rows=WIDE):
    return lax.broadcasted_iota(jnp.int32, (rows, DEPTH), 1) == k


def table_of(i):
    if i >= 24:
        return i - 6
    if i >= 19:
        return i - 20
    return i - 1


def add_all(values):
    total = values[0]
    for value in values[1:]:
        total = total + value
    return total


def signed_sum(terms):
    total = None
    for sign, value in terms:
        if total is None:
            total = value if sign > 0 else -value
        else:
            total = total + value if sign > 0 else total - value
    return total


def moments(s):
    diff = {}
    parts = [s[0]]
    for i, j in FLOW_PAIRS:
        parts.append(s[i] + s[j])
        diff[i] = s[i] - s[j]
    density = add_all(parts)
    speed = []
    for axis in range(3):
        speed.append(signed_sum([(VEL[i][axis], diff[i]) for i, _ in FLOW_PAIRS if VEL[i][axis]]))
    temper = add_all([s[i] for i in range(19, 26)])
    return density, speed, temper


def collided(s, density, speed, temper):
    ux, uy, uz = speed
    vz = uz + LIFT * (temper - MEAN_TEMP)
    vel = (ux, uy, vz)
    base = density - 1.5 * (ux * ux + uy * uy + vz * vz)
    out = [None] * 26
    out[0] = KEEP * s[0] + (INV_TAU * weight(0)) * base
    for i, j in FLOW_PAIRS:
        proj = signed_sum([(VEL[i][a], vel[a]) for a in range(3) if VEL[i][a]])
        factor = INV_TAU * weight(i)
        even = factor * base + (4.5 * factor) * (proj * proj)
        odd = (3.0 * factor) * proj
        out[i] = KEEP * s[i] + (even + odd)
        out[j] = KEEP * s[j] + (even - odd)
    out[19] = KEEP * s[19] + (INV_TAU * weight(19)) * temper
    scaled = (INV_TAU * weight(20)) * temper
    for (i, j), u in zip(HEAT_PAIRS, (ux, uy, uz)):
        odd = scaled * (4.0 * u)
        out[i] = KEEP * s[i] + (scaled + odd)
        out[j] = KEEP * s[j] + (scaled - odd)
    return out


def pack_kernel(place, plane, *refs):
    outs, tall = refs[:8], refs[8]

    def fill(c):
        tall[c, 0:4] = plane[c, 60:64]
        tall[c, 4:68] = plane[c]
        tall[c, 68:72] = plane[c, 0:4]

    loop(26, fill)
    for k in range(8):
        base = pl.multiple_of(OWN * lax.rem(place[0] + k, 8), 8)

        def one(c, k=k, base=base):
            outs[k][c] = tall[c, pl.ds(base, WIDE)]

        loop(26, one)


def table_kernel(region, table):
    first = lane_is(0)
    last = lane_is(DEPTH - 1)

    def one(n):
        at = At(n, 1)
        x = at.by(0)
        for i in range(1, 19):
            cx, cy, cz = VEL[i]
            value = shifted(region[0, at.by(-cx)], cy, cz)
            if cz:
                edge = first if cz > 0 else last
                if i in (5, 6):
                    table[x, table_of(i + 19)] = jnp.where(edge, -1.0, value)
                value = jnp.where(edge, 1.0, value)
            table[x, table_of(i)] = value

    loop(WIDE - 2, one)


def streamed(p, table, at):
    x = at.by(0)
    s = []
    for i in range(26):
        if i in (0, 19):
            s.append(p[x, i])
            continue
        cx, cy, cz = VEL[i]
        moved = shifted(p[at.by(-cx), i], cy, cz)
        t = table[x, table_of(i)]
        back = p[x, OPP[i]]
        if i >= 24:
            back = t * back
        s.append(jnp.where(t == 0.0, moved, back))
    return s


def forward_kernel(place, *refs):
    planes, halos = refs[:8], refs[8:16]
    table, region, mom, edge, edge_lo, edge_hi, heat, pa, pb, mom3 = refs[16:]
    first = lane_is(0)

    def start(src, x):
        s = [src[i] for i in range(26)]
        density, speed, temper = moments(s)
        for a, value in enumerate((*speed, temper)):
            mom[0, x, a] = value
        for i, value in enumerate(collided(s, density, speed, temper)):
            pa[x, i] = value

    for k in range(8):
        n = lax.rem(place[0] + (8 - k), 8)
        start(planes[k], n + HALO)
        start(halos[k], jnp.where(n >= HALO, n - HALO, n + OWN + HALO))

    def arrive(p, at):
        s = streamed(p, table, at)
        s[RISING] = s[RISING] + jnp.where(first, 0.25 * region[1, at.by(0)], 0.0)
        return s

    src, dst = pa, pb
    for k in range(1, 4):

        def one(n, k=k, src=src, dst=dst):
            at = At(n, k)
            x = at.by(0)
            s = arrive(src, at)
            density, speed, temper = moments(s)
            for a, value in enumerate((*speed, temper)):
                if k < 3:
                    mom[k, x, a] = value
                else:
                    mom3[x, a] = value
            for i, value in enumerate(collided(s, density, speed, temper)):
                dst[x, i] = value

        loop(WIDE - 2 * k, one)
        src, dst = dst, src

    heat[...] = jnp.zeros_like(heat)

    def last(n):
        at = At(n, HALO)
        x = at.by(0)
        s = arrive(src, at)
        _, speed, temper = moments(s)
        values = [mom3[x, a] for a in range(4)] + [speed[2], temper]
        for a, value in enumerate(values):
            edge[n, a] = value[4:12]
            edge_lo[n, a] = value[4:8]
            edge_hi[n, a] = value[8:12]
        flux = (1.0 - region[0, x]) * speed[2] * temper
        heat[...] += flux[4:12]

    loop(OWN, last)


def adjoint_cell(lam, table, at, base, fluids, vel, temper):
    x = at.by(0)
    fluid, fluid_up, fluid_down = fluids
    ux, uy, uz = vel
    vz = uz + LIFT * (temper - MEAN_TEMP)
    v = (ux, uy, vz)

    def mu_of(j):
        cx, cy, cz = VEL[j]
        if j in (0, 19):
            return lam[at.by(-base), j]
        moved = shifted(lam[at.by(cx - base), j], -cy, -cz)
        keep = fluid if cz == 0 else (fluid_up if cz > 0 else fluid_down)
        return keep * moved + table[x, table_of(OPP[j])] * lam[at.by(-base), OPP[j]]

    mu = [mu_of(j) for j in range(26)]
    axis_sum = add_all([mu[i] + mu[j] for i, j in FLOW_PAIRS[:3]])
    pair_sum = {i: mu[i] + mu[j] for i, j in FLOW_PAIRS}
    pair_diff = {i: mu[i] - mu[j] for i, j in FLOW_PAIRS}
    wa, wd = weight(1), weight(7)
    diag = add_all([pair_sum[i] for i, _ in FLOW_PAIRS[3:]])
    zeroth = weight(0) * mu[0] + wa * axis_sum + wd * diag

    def first(a):
        axis = 1 + 2 * a
        rest = signed_sum([(VEL[i][a], pair_diff[i]) for i, _ in FLOW_PAIRS[3:] if VEL[i][a]])
        return wa * pair_diff[axis] + wd * rest

    def second(a, b):
        if a == b:
            rest = add_all([pair_sum[i] for i, _ in FLOW_PAIRS[3:] if VEL[i][a]])
            return wa * pair_sum[1 + 2 * a] + wd * rest
        return wd * signed_sum(
            [(VEL[i][a] * VEL[i][b], pair_sum[i]) for i, _ in FLOW_PAIRS[3:] if VEL[i][a] * VEL[i][b]]
        )

    m2 = {(a, b): second(a, b) for a in range(3) for b in range(a, 3)}
    force = []
    for a in range(3):
        bent = add_all([m2[min(a, b), max(a, b)] * v[b] for b in range(3)])
        force.append(3.0 * first(a) + 9.0 * bent - 3.0 * (v[a] * zeroth))
    heat_diff = [mu[i] - mu[j] for i, j in HEAT_PAIRS]
    heat_even = weight(19) * mu[19] + weight(20) * add_all([mu[i] + mu[j] for i, j in HEAT_PAIRS])
    wh = 4.0 * weight(20)
    heat_odd = add_all([heat_diff[a] * (wh * u) for a, u in enumerate((ux, uy, uz))])
    to_heat = INV_TAU * (LIFT * force[2] + heat_even + heat_odd)
    scaled = wh * temper
    pull = [INV_TAU * (force[a] + scaled * heat_diff[a]) for a in range(3)]
    base = INV_TAU * zeroth
    out = [None] * 26
    out[0] = KEEP * mu[0] + base
    for i, j in FLOW_PAIRS:
        proj = signed_sum([(VEL[i][a], pull[a]) for a in range(3) if VEL[i][a]])
        out[i] = KEEP * mu[i] + (base + proj)
        out[j] = KEEP * mu[j] + (base - proj)
    for i in range(19, 26):
        out[i] = KEEP * mu[i] + to_heat
    return out


def merge_kernel(lo, mid, hi, head, tail):
    for n in range(HALO):
        for out, x in ((head, n), (tail, n + HALO)):
            for a in range(6):
                out[n, a, 0:4] = lo[x, a]
                out[n, a, 4:12] = mid[x, a]
                out[n, a, 12:16] = hi[x, a]


def adjoint_planes(k, state_of, bufs, table, region, put, base):
    first = lane_is(0)
    last = lane_is(DEPTH - 1)

    def one(n):
        at = At(n, HALO - k)
        x = at.by(0)
        fluid = 1.0 - region[0, x]
        fluids = (fluid, jnp.where(last, 0.0, fluid), jnp.where(first, 0.0, fluid))
        state = [state_of(x, a) for a in range(4)]
        for chain, src in enumerate(bufs):
            lam = adjoint_cell(src, table, at, base, fluids, state[:3], state[3])
            for i in range(26):
                put(chain, n, x, i, lam[i])

    loop(OWN + 2 * k, one)


def backward_kernel(*refs):
    own, gl, gr, slo, shi, elo, emid, ehi, el, er, mom, table, region, row = refs[:14]
    end_a, end_b, slots, la0, la1, lb0, lb1, late, sums = refs[14:]

    def gather(src, count, off):
        def one(x):
            for i in range(26):
                la0[x + off, i, 0:4] = slo[i, x + off]
                la0[x + off, i, 4:12] = src[i, x]
                la0[x + off, i, 12:16] = shi[i, x + off]

        loop(count, one)

    gather(gl, HALO, 0)
    gather(own, OWN, HALO)
    gather(gr, HALO, HALO + OWN)

    def settle(x):
        for a in range(6):
            late[x + HALO, a, 0:4] = elo[x, a]
            late[x + HALO, a, 4:12] = emid[x, a]
            late[x + HALO, a, 12:16] = ehi[x, a]

    loop(OWN, settle)

    def flank(x):
        for a in range(6):
            late[x, a] = el[x, a]
            late[x + HALO + OWN, a] = er[x, a]

    loop(HALO, flank)

    def seed(x):
        fluid = 1.0 - region[0, x]
        up = fluid * late[x, 5]
        zero = jnp.zeros_like(up)
        heat = fluid * late[x, 4]
        for i in range(26):
            cz = VEL[i][2]
            lb0[x, i] = heat if i >= 19 else (zero if cz == 0 else (up if cz > 0 else -up))

    loop(WIDE, seed)

    def collect(chain, lam, fresh, base):
        for n in range(OWN):
            value = lam[n + HALO - base, RISING][4:12]
            spot = pl.ds(OWN * OWN * chain + OWN * n, OWN)
            sums[spot] = value if fresh else sums[spot] + value

    bufs = [(la0, la1), (lb0, lb1)]
    for k in (3, 2, 1):
        for chain, (src, _) in enumerate(bufs):
            collect(chain, src, k == 3, 0)

        def put(chain, n, x, i, value, k=k, dsts=(bufs[0][1], bufs[1][1])):
            if k == 1:
                (end_a, end_b)[chain][n, i] = value
            else:
                dsts[chain][x, i] = value

        def state_of(x, a, k=k):
            return late[x, a] if k == 3 else mom[k, x, a]

        adjoint_planes(k, state_of, [src for src, _ in bufs], table, region, put, 0)
        bufs = [(dst, src) for src, dst in bufs]
    collect(0, end_a, False, HALO - 1)
    collect(1, end_b, False, HALO - 1)

    line = 0.25 * jnp.transpose(sums[...])[0:1]
    pair = jnp.concatenate([line, row[...]], 0)
    count = slots.shape[0]

    def spread(n):
        for q in range(8):
            slots[8 * n + q] = pair

    loop(count // 8, spread)


def final_kernel(end_a, end_b, mom, table, region, out_a, out_b):
    def put(chain, n, x, i, value):
        (out_a, out_b)[chain][i, n] = value[4:12]

    adjoint_planes(
        0, lambda x, a: mom[0, x, a], [end_a, end_b], table, region, put, HALO - 1
    )


def split3(value):
    high = value.astype(jnp.bfloat16)
    rest = value - high.astype(jnp.float32)
    mid = rest.astype(jnp.bfloat16)
    low = (rest - mid.astype(jnp.float32)).astype(jnp.bfloat16)
    return high, mid, low


def tile_kernel(scale, told, theta, first, second, theta_new, first_new, second_new, nusselt):
    rows = told.shape[0] // 2
    half = DEPTH // 2
    lane = lax.broadcasted_iota(jnp.int32, (8, DEPTH), 1)
    left = lane < half

    def flux(r, total):
        return total + told[pl.ds(pl.multiple_of(8 * r, 8), 8)]

    total = lax.fori_loop(0, rows // 4, flux, jnp.zeros((8, DEPTH), jnp.float32))
    odd = lax.rem(lax.broadcasted_iota(jnp.int32, (8, DEPTH), 0), 2) == 1
    share = jnp.sum(jnp.where(odd & (lane == half), total, 0.0)) * scale[0]
    nusselt[0, 0] = 1.0 + share

    def one(r, total):
        base = pl.multiple_of(32 * r, 32)
        even_grad = told[pl.ds(base, 8, stride=4)]
        even_name = told[pl.ds(base + 1, 8, stride=4)]
        odd_grad = told[pl.ds(base + 2, 8, stride=4)]
        odd_name = told[pl.ds(base + 3, 8, stride=4)]

        def whole(pair):
            return pair + share * pltpu.roll(pair, half, 1)

        value = jnp.where(left, whole(even_grad), pltpu.roll(whole(odd_grad), half, 1))
        ident = jnp.where(left, even_name, pltpu.roll(odd_name, half, 1)).astype(jnp.int32)
        upper = ident // DEPTH
        lower = ident - upper * DEPTH
        pieces = [piece.astype(jnp.float32) for piece in split3(value)]
        high_is = lax.broadcasted_iota(jnp.int32, (32, DEPTH), 0)
        low_is = lax.broadcasted_iota(jnp.int32, (DEPTH, DEPTH), 0)
        lhs, rhs = [], []
        for q in range(8):
            hot = high_is == jnp.broadcast_to(upper[q : q + 1], (32, DEPTH))
            lhs.append(
                jnp.concatenate(
                    [
                        jnp.where(hot, jnp.broadcast_to(piece[q : q + 1], (32, DEPTH)), 0.0)
                        for piece in pieces
                    ],
                    0,
                ).astype(jnp.bfloat16)
            )
            hot = low_is == jnp.broadcast_to(lower[q : q + 1], (DEPTH, DEPTH))
            rhs.append(jnp.where(hot, 1.0, 0.0).astype(jnp.bfloat16))
        return total + lax.dot_general(
            jnp.concatenate(lhs, 1),
            jnp.concatenate(rhs, 1),
            (((1,), (1,)), ((), ())),
            preferred_element_type=jnp.float32,
        )

    total = lax.fori_loop(0, rows // 16, one, jnp.zeros((96, DEPTH), jnp.float32))
    grad = (total[0:32] + total[32:64]) + total[64:96]
    new_first = BETA_ONE * first[...] + (1.0 - BETA_ONE) * grad
    new_second = BETA_TWO * second[...] + (1.0 - BETA_TWO) * grad * grad
    first_hat = new_first / (1.0 - BETA_ONE**ADAM_STEP)
    second_hat = new_second / (1.0 - BETA_TWO**ADAM_STEP)
    theta_new[...] = theta[...] - LEARN_RATE * first_hat / (jnp.sqrt(second_hat) + ADAM_EPS)
    first_new[...] = new_first
    second_new[...] = new_second


def neighbour(value, axis, step):
    count = lax.axis_size(axis)
    return lax.ppermute(value, axis, [(i, (i + step) % count) for i in range(count)])


def forward_gx(value, k):
    count, group = lax.axis_size("gx"), lax.axis_size("st")
    pairs = []
    for g in range(count):
        for s in range(group):
            to = g + 1 if (s - k) % group >= HALO else g - 1
            pairs.append((g * group + s, (to % count) * group + s))
    return lax.ppermute(value, ("gx", "st"), pairs)


def after(value, *earlier):
    return lax.optimization_barrier((value, *earlier))[0]


def body(checkpoint, adjoint_in, solid_mask, tile_map, theta, first_moment, second_moment):
    vmem = pltpu.VMEM
    f32 = jnp.float32
    place = lax.axis_index("st").astype(jnp.int32).reshape(1)
    packed = call(
        pack_kernel, [(26, WIDE, DEPTH)] * 8, [vmem((26, 72, DEPTH), f32)], 12, 1, 2
    )(place, checkpoint[:, 0])

    plate = jnp.broadcast_to(theta[tile_map][:, :, None], (OWN, OWN, DEPTH))
    flags = jnp.stack([solid_mask.astype(f32), plate])
    low = neighbour(flags[:, 4:8], "gx", 1)
    high = neighbour(flags[:, 0:4], "gx", -1)
    flags = jnp.concatenate([low, flags, high], 1)
    low = neighbour(flags[:, :, 4:8], "st", 1)
    high = neighbour(flags[:, :, 0:4], "st", -1)
    region = jnp.concatenate([low, flags, high], 2)
    table = call(table_kernel, [(WIDE, 20, WIDE, DEPTH)], mib=8)(region)[0]

    planes = [packed[0]] + [None] * 7
    for k in (1, 7, 2, 6, 3, 5, 4):
        planes[k] = neighbour(packed[k], "st", k)
    halos = [forward_gx(planes[k], k) for k in range(8)]

    mine = after(adjoint_in, flags)
    gl = neighbour(mine[:, 4:8], "gx", 1)
    gr = neighbour(mine[:, 0:4], "gx", -1)
    tall = after(jnp.concatenate([gl, adjoint_in, gr], 1), planes[4])
    slo = neighbour(tall[:, :, 4:8], "st", 1)
    shi = neighbour(tall[:, :, 0:4], "st", -1)

    big = (WIDE, 26, WIDE, DEPTH)
    mom, edge, edge_lo, edge_hi, heat = call(
        forward_kernel,
        [(3, WIDE, 4, WIDE, DEPTH), (OWN, 6, OWN, DEPTH), (OWN, 6, 4, DEPTH), (OWN, 6, 4, DEPTH), (OWN, DEPTH)],
        [vmem(big, f32), vmem(big, f32), vmem((WIDE, 4, WIDE, DEPTH), f32)],
        20,
        1,
        19,
    )(place, *planes, *halos, table, region)
    elo = neighbour(edge_hi, "st", 1)
    ehi = neighbour(edge_lo, "st", -1)
    head, tail = call(merge_kernel, [(HALO, 6, WIDE, DEPTH)] * 2, mib=4)(elo, edge, ehi)
    el = neighbour(tail, "gx", 1)
    er = neighbour(head, "gx", -1)

    count = lax.axis_size("gx") * lax.axis_size("st")
    row = jnp.concatenate(
        [tile_map.reshape(1, -1).astype(f32), jnp.broadcast_to(jnp.sum(heat), (1, OWN * OWN))], 1
    )
    near = (OWN + 2, 26, WIDE, DEPTH)
    end_a, end_b, slots = call(
        backward_kernel,
        [near, near, (count, 2, DEPTH)],
        [vmem(big, f32)] * 4 + [vmem((WIDE, 6, WIDE, DEPTH), f32), vmem((DEPTH, DEPTH), f32)],
        32,
    )(adjoint_in, gl, gr, slo, shi, elo, edge, ehi, el, er, mom, table, region, row)
    told = lax.all_to_all(slots, ("gx", "st"), 0, 0, tiled=True)
    out_a, out_b = call(final_kernel, [(26, OWN, OWN, DEPTH)] * 2, mib=16)(
        end_a, end_b, mom, table, region
    )

    scale = jnp.full((1,), 1.0 / (KAPPA * count * OWN * OWN), f32)
    tiles = (theta.shape[0] // DEPTH, DEPTH)
    theta_new, first_new, second_new, nusselt = call(
        tile_kernel,
        [tiles] * 3 + [(1, 1)],
        mib=8,
        scalars=1,
        inputs=5,
        out_specs=[pltpu.VMEM] * 3 + [pltpu.SMEM],
    )(
        scale,
        told.reshape(2 * count, DEPTH),
        theta.reshape(tiles),
        first_moment.reshape(tiles),
        second_moment.reshape(tiles),
    )
    nusselt = nusselt.reshape(())
    adjoint = out_a + (nusselt - 1.0) * out_b
    flat = theta.shape
    return (adjoint, theta_new.reshape(flat), first_new.reshape(flat), second_new.reshape(flat), nusselt)


def solution(mesh):
    return jax.shard_map(
        body,
        mesh=mesh,
        in_specs=(
            P(None, ("gx", "st"), None, None),
            P(None, "gx", "st", None),
            P("gx", "st", None),
            P("gx", "st"),
            P(),
            P(),
            P(),
        ),
        out_specs=(P(None, "gx", "st", None), P(), P(), P(), P()),
        check_vma=False,
    )
```

```python
import jax
import jax.numpy as jnp
import numpy as np
from jax import lax
from jax.experimental import pallas as pl
from jax.experimental.pallas import tpu as pltpu
from jax.sharding import PartitionSpec as P


ADAM_STEP = 100

VELOCITY = np.array(
    [
        [0, 0, 0],
        [1, 0, 0],
        [-1, 0, 0],
        [0, 1, 0],
        [0, -1, 0],
        [0, 0, 1],
        [0, 0, -1],
        [1, 1, 0],
        [-1, -1, 0],
        [1, -1, 0],
        [-1, 1, 0],
        [1, 0, 1],
        [-1, 0, -1],
        [1, 0, -1],
        [-1, 0, 1],
        [0, 1, 1],
        [0, -1, -1],
        [0, 1, -1],
        [0, -1, 1],
        [0, 0, 0],
        [1, 0, 0],
        [-1, 0, 0],
        [0, 1, 0],
        [0, -1, 0],
        [0, 0, 1],
        [0, 0, -1],
    ],
    dtype=np.int32,
)
VEL = [tuple(int(v) for v in row) for row in VELOCITY]
OPP = [0, 2, 1, 4, 3, 6, 5, 8, 7, 10, 9, 12, 11, 14, 13, 16, 15, 18, 17, 19, 21, 20, 23, 22, 25, 24]
FLOW_PAIRS = [(i, i + 1) for i in range(1, 19, 2)]
HEAT_PAIRS = [(20, 21), (22, 23), (24, 25)]
INV_TAU = 1.25
KEEP = 1.0 - INV_TAU
LIFT = 0.8 * 0.001
MEAN_TEMP = 0.5
KAPPA = 0.075
RISING = 24
LEARN_RATE = 0.05
BETA_ONE = 0.9
BETA_TWO = 0.99
ADAM_EPS = 1e-08

HALO = 4
OWN = 8
WIDE = OWN + 2 * HALO
DEPTH = 128
INTERPRET = False


def weight(i):
    if i < 19:
        return 1.0 / 3.0 if i == 0 else (1.0 / 18.0 if i < 7 else 1.0 / 36.0)
    return 0.25 if i == 19 else 0.125


def call(kernel, outs, scratch=(), mib=8, scalars=0, inputs=None, out_specs=None, in_specs=None):
    extra = {}
    if in_specs:
        extra["in_specs"] = [pl.BlockSpec(memory_space=space) for space in in_specs]
    if scalars:
        extra["in_specs"] = [pl.BlockSpec(memory_space=pltpu.SMEM)] * scalars + [
            pl.BlockSpec(memory_space=pltpu.VMEM)
        ] * (inputs - scalars)
    if out_specs:
        extra["out_specs"] = [pl.BlockSpec(memory_space=space) for space in out_specs]
    return pl.pallas_call(
        kernel,
        out_shape=[jax.ShapeDtypeStruct(s, jnp.float32) for s in outs],
        scratch_shapes=list(scratch),
        compiler_params=pltpu.CompilerParams(vmem_limit_bytes=mib << 20),
        interpret=INTERPRET,
        **extra,
    )


class At:
    def __init__(self, index, offset):
        self.index, self.offset = index, offset

    def by(self, more):
        return self.index + (self.offset + more) if self.offset + more else self.index


def loop(count, fn):
    lax.fori_loop(0, count, lambda i, c: (fn(i), c)[1], 0)


def shifted(value, step_y, step_z):
    if step_y:
        value = pltpu.roll(value, step_y % value.shape[0], 0)
    if step_z:
        value = pltpu.roll(value, step_z % DEPTH, 1)
    return value


def lane_is(k, rows=WIDE):
    return lax.broadcasted_iota(jnp.int32, (rows, DEPTH), 1) == k


def table_of(i):
    if i >= 24:
        return i - 6
    if i >= 19:
        return i - 20
    return i - 1


def add_all(values):
    total = values[0]
    for value in values[1:]:
        total = total + value
    return total


def signed_sum(terms):
    total = None
    for sign, value in terms:
        if total is None:
            total = value if sign > 0 else -value
        else:
            total = total + value if sign > 0 else total - value
    return total


def moments(s):
    diff = {}
    parts = [s[0]]
    for i, j in FLOW_PAIRS:
        parts.append(s[i] + s[j])
        diff[i] = s[i] - s[j]
    density = add_all(parts)
    speed = []
    for axis in range(3):
        speed.append(signed_sum([(VEL[i][axis], diff[i]) for i, _ in FLOW_PAIRS if VEL[i][axis]]))
    temper = add_all([s[i] for i in range(19, 26)])
    return density, speed, temper


def collided(s, density, speed, temper):
    ux, uy, uz = speed
    vz = uz + LIFT * (temper - MEAN_TEMP)
    vel = (ux, uy, vz)
    base = density - 1.5 * (ux * ux + uy * uy + vz * vz)
    out = [None] * 26
    out[0] = KEEP * s[0] + (INV_TAU * weight(0)) * base
    for i, j in FLOW_PAIRS:
        proj = signed_sum([(VEL[i][a], vel[a]) for a in range(3) if VEL[i][a]])
        factor = INV_TAU * weight(i)
        even = factor * base + (4.5 * factor) * (proj * proj)
        odd = (3.0 * factor) * proj
        out[i] = KEEP * s[i] + (even + odd)
        out[j] = KEEP * s[j] + (even - odd)
    out[19] = KEEP * s[19] + (INV_TAU * weight(19)) * temper
    scaled = (INV_TAU * weight(20)) * temper
    for (i, j), u in zip(HEAT_PAIRS, (ux, uy, uz)):
        odd = scaled * (4.0 * u)
        out[i] = KEEP * s[i] + (scaled + odd)
        out[j] = KEEP * s[j] + (scaled - odd)
    return out


def pack_kernel(place, plane, *refs):
    outs, tall = refs[:8], refs[8]

    def fill(c):
        tall[c, 0:4] = plane[c, 60:64]
        tall[c, 4:68] = plane[c]
        tall[c, 68:72] = plane[c, 0:4]

    loop(26, fill)
    for k in range(8):
        base = pl.multiple_of(OWN * lax.rem(place[0] + k, 8), 8)

        def one(c, k=k, base=base):
            outs[k][c] = tall[c, pl.ds(base, WIDE)]

        loop(26, one)


def table_kernel(region, table):
    first = lane_is(0)
    last = lane_is(DEPTH - 1)

    def one(n):
        at = At(n, 1)
        x = at.by(0)
        for i in range(1, 19):
            cx, cy, cz = VEL[i]
            value = shifted(region[0, at.by(-cx)], cy, cz)
            if cz:
                edge = first if cz > 0 else last
                if i in (5, 6):
                    table[x, table_of(i + 19)] = jnp.where(edge, -1.0, value)
                value = jnp.where(edge, 1.0, value)
            table[x, table_of(i)] = value

    loop(WIDE - 2, one)


def streamed(p, table, at):
    x = at.by(0)
    s = []
    for i in range(26):
        if i in (0, 19):
            s.append(p[x, i])
            continue
        cx, cy, cz = VEL[i]
        moved = shifted(p[at.by(-cx), i], cy, cz)
        t = table[x, table_of(i)]
        back = p[x, OPP[i]]
        if i >= 24:
            back = t * back
        s.append(jnp.where(t == 0.0, moved, back))
    return s


def forward_kernel(place, *refs):
    planes, halos = refs[:8], refs[8:16]
    table, region, mom, edge, edge_lo, edge_hi, heat, pa, pb, mom3 = refs[16:]
    first = lane_is(0)

    def start(src, x):
        s = [src[i] for i in range(26)]
        density, speed, temper = moments(s)
        for a, value in enumerate((*speed, temper)):
            mom[0, x, a] = value
        for i, value in enumerate(collided(s, density, speed, temper)):
            pa[x, i] = value

    for k in range(8):
        n = lax.rem(place[0] + (8 - k), 8)
        start(planes[k], n + HALO)
        start(halos[k], jnp.where(n >= HALO, n - HALO, n + OWN + HALO))

    def arrive(p, at):
        s = streamed(p, table, at)
        s[RISING] = s[RISING] + jnp.where(first, 0.25 * region[1, at.by(0)], 0.0)
        return s

    src, dst = pa, pb
    for k in range(1, 4):

        def one(n, k=k, src=src, dst=dst):
            at = At(n, k)
            x = at.by(0)
            s = arrive(src, at)
            density, speed, temper = moments(s)
            for a, value in enumerate((*speed, temper)):
                if k < 3:
                    mom[k, x, a] = value
                else:
                    mom3[x, a] = value
            for i, value in enumerate(collided(s, density, speed, temper)):
                dst[x, i] = value

        loop(WIDE - 2 * k, one)
        src, dst = dst, src

    def last(n, total):
        at = At(n, HALO)
        x = at.by(0)
        s = arrive(src, at)
        _, speed, temper = moments(s)
        values = [mom3[x, a] for a in range(4)] + [speed[2], temper]
        for a, value in enumerate(values):
            edge[n, a] = value[4:12]
            edge_lo[n, a] = value[4:8]
            edge_hi[n, a] = value[8:12]
        flux = (1.0 - region[0, x]) * speed[2] * temper
        return total + flux[4:12]

    total = lax.fori_loop(0, OWN, last, jnp.zeros((OWN, DEPTH), jnp.float32))
    heat[...] = jnp.broadcast_to(jnp.sum(total), heat.shape)


def adjoint_cell(lam, table, at, fluids, vel, temper):
    x = at.by(0)
    fluid, fluid_up, fluid_down = fluids
    ux, uy, uz = vel
    vz = uz + LIFT * (temper - MEAN_TEMP)
    v = (ux, uy, vz)

    def mu_of(j):
        cx, cy, cz = VEL[j]
        if j in (0, 19):
            return lam[x, j]
        moved = shifted(lam[at.by(cx), j], -cy, -cz)
        keep = fluid if cz == 0 else (fluid_up if cz > 0 else fluid_down)
        return keep * moved + table[x, table_of(OPP[j])] * lam[x, OPP[j]]

    mu = [mu_of(j) for j in range(26)]
    axis_sum = add_all([mu[i] + mu[j] for i, j in FLOW_PAIRS[:3]])
    pair_sum = {i: mu[i] + mu[j] for i, j in FLOW_PAIRS}
    pair_diff = {i: mu[i] - mu[j] for i, j in FLOW_PAIRS}
    wa, wd = weight(1), weight(7)
    diag = add_all([pair_sum[i] for i, _ in FLOW_PAIRS[3:]])
    zeroth = weight(0) * mu[0] + wa * axis_sum + wd * diag

    def first(a):
        axis = 1 + 2 * a
        rest = signed_sum([(VEL[i][a], pair_diff[i]) for i, _ in FLOW_PAIRS[3:] if VEL[i][a]])
        return wa * pair_diff[axis] + wd * rest

    def second(a, b):
        if a == b:
            rest = add_all([pair_sum[i] for i, _ in FLOW_PAIRS[3:] if VEL[i][a]])
            return wa * pair_sum[1 + 2 * a] + wd * rest
        return wd * signed_sum(
            [(VEL[i][a] * VEL[i][b], pair_sum[i]) for i, _ in FLOW_PAIRS[3:] if VEL[i][a] * VEL[i][b]]
        )

    m2 = {(a, b): second(a, b) for a in range(3) for b in range(a, 3)}
    force = []
    for a in range(3):
        bent = add_all([m2[min(a, b), max(a, b)] * v[b] for b in range(3)])
        force.append(3.0 * first(a) + 9.0 * bent - 3.0 * (v[a] * zeroth))
    heat_diff = [mu[i] - mu[j] for i, j in HEAT_PAIRS]
    heat_even = weight(19) * mu[19] + weight(20) * add_all([mu[i] + mu[j] for i, j in HEAT_PAIRS])
    wh = 4.0 * weight(20)
    heat_odd = add_all([heat_diff[a] * (wh * u) for a, u in enumerate((ux, uy, uz))])
    to_heat = INV_TAU * (LIFT * force[2] + heat_even + heat_odd)
    scaled = wh * temper
    pull = [INV_TAU * (force[a] + scaled * heat_diff[a]) for a in range(3)]
    base = INV_TAU * zeroth
    out = [None] * 26
    out[0] = KEEP * mu[0] + base
    for i, j in FLOW_PAIRS:
        proj = signed_sum([(VEL[i][a], pull[a]) for a in range(3) if VEL[i][a]])
        out[i] = KEEP * mu[i] + (base + proj)
        out[j] = KEEP * mu[j] + (base - proj)
    for i in range(19, 26):
        out[i] = KEEP * mu[i] + to_heat
    return out


def merge_kernel(lo, mid, hi, head, tail):
    for n in range(HALO):
        for out, x in ((head, n), (tail, n + HALO)):
            for a in range(6):
                out[n, a, 0:4] = lo[x, a]
                out[n, a, 4:12] = mid[x, a]
                out[n, a, 12:16] = hi[x, a]


def adjoint_planes(k, state_of, bufs, table, region, put):
    first = lane_is(0)
    last = lane_is(DEPTH - 1)

    def one(n):
        at = At(n, HALO - k)
        x = at.by(0)
        fluid = 1.0 - region[0, x]
        fluids = (fluid, jnp.where(last, 0.0, fluid), jnp.where(first, 0.0, fluid))
        state = [state_of(x, a) for a in range(4)]
        for chain, src in enumerate(bufs):
            lam = adjoint_cell(src, table, at, fluids, state[:3], state[3])
            for i in range(26):
                put(chain, n, x, i, lam[i])

    loop(OWN + 2 * k, one)


def backward_kernel(*refs):
    own, gl, gr, slo, shi, elo, emid, ehi, el, er, mom, table, region, names, heat = refs[:15]
    out_a, out_b, slots, la0, la1, lb0, lb1, late, sums, last_a, last_b, sems = refs[15:]

    def gather(src, count, off):
        def one(x):
            for i in range(26):
                la0[x + off, i, 0:4] = slo[i, x + off]
                la0[x + off, i, 4:12] = src[i, x]
                la0[x + off, i, 12:16] = shi[i, x + off]

        loop(count, one)

    gather(gl, HALO, 0)
    gather(own, OWN, HALO)
    gather(gr, HALO, HALO + OWN)

    def settle(x):
        for a in range(6):
            late[x + HALO, a, 0:4] = elo[x, a]
            late[x + HALO, a, 4:12] = emid[x, a]
            late[x + HALO, a, 12:16] = ehi[x, a]

    loop(OWN, settle)

    def flank(x):
        for a in range(6):
            late[x, a] = el[x, a]
            late[x + HALO + OWN, a] = er[x, a]

    loop(HALO, flank)

    def seed(x):
        fluid = 1.0 - region[0, x]
        up = fluid * late[x, 5]
        zero = jnp.zeros_like(up)
        heat = fluid * late[x, 4]
        for i in range(26):
            cz = VEL[i][2]
            lb0[x, i] = heat if i >= 19 else (zero if cz == 0 else (up if cz > 0 else -up))

    loop(WIDE, seed)

    def collect(chain, lam, fresh):
        for n in range(OWN):
            value = lam[n + HALO, RISING][4:12]
            spot = pl.ds(OWN * OWN * chain + OWN * n, OWN)
            sums[spot] = value if fresh else sums[spot] + value

    bufs = [(la0, la1), (lb0, lb1)]
    for k in (3, 2, 1, 0):
        for chain, (src, _) in enumerate(bufs):
            collect(chain, src, k == 3)

        def put(chain, n, x, i, value, k=k, dsts=(bufs[0][1], bufs[1][1])):
            if k == 0:
                (last_a, last_b)[chain][i, n] = value[4:12]
            else:
                dsts[chain][x, i] = value

        def state_of(x, a, k=k):
            return late[x, a] if k == 3 else mom[k, x, a]

        adjoint_planes(k, state_of, [src for src, _ in bufs], table, region, put)
        bufs = [(dst, src) for src, dst in bufs]
    copies = [
        pltpu.make_async_copy(last_a, out_a, sems.at[0]),
        pltpu.make_async_copy(last_b, out_b, sems.at[1]),
    ]
    for copy in copies:
        copy.start()

    line = 0.25 * jnp.transpose(sums[...])[0:1]
    lane = lax.broadcasted_iota(jnp.int32, (1, DEPTH), 1)
    pair = jnp.concatenate([line, jnp.where(lane < OWN * OWN, names[...], heat[...])], 0)
    count = slots.shape[0]

    def spread(n):
        for q in range(8):
            slots[8 * n + q] = pair

    loop(count // 8, spread)
    for copy in copies:
        copy.wait()


def split3(value):
    high = value.astype(jnp.bfloat16)
    rest = value - high.astype(jnp.float32)
    mid = rest.astype(jnp.bfloat16)
    low = (rest - mid.astype(jnp.float32)).astype(jnp.bfloat16)
    return high, mid, low


def tile_kernel(
    scale, told, theta, first, second, part_a, part_b, theta_new, first_new, second_new, nusselt, adjoint, va, vb, sems
):
    copies = [
        pltpu.make_async_copy(part_a, va, sems.at[0]),
        pltpu.make_async_copy(part_b, vb, sems.at[1]),
    ]
    for copy in copies:
        copy.start()
    rows = told.shape[0] // 2
    half = DEPTH // 2
    lane = lax.broadcasted_iota(jnp.int32, (8, DEPTH), 1)
    left = lane < half

    def flux(r, total):
        return total + told[pl.ds(pl.multiple_of(8 * r, 8), 8)]

    total = lax.fori_loop(0, rows // 4, flux, jnp.zeros((8, DEPTH), jnp.float32), unroll=8)
    odd = lax.rem(lax.broadcasted_iota(jnp.int32, (8, DEPTH), 0), 2) == 1
    share = jnp.sum(jnp.where(odd & (lane == half), total, 0.0)) * scale[0]
    nusselt[0, 0] = 1.0 + share

    def one(r, total):
        base = pl.multiple_of(32 * r, 32)
        even_grad = told[pl.ds(base, 8, stride=4)]
        even_name = told[pl.ds(base + 1, 8, stride=4)]
        odd_grad = told[pl.ds(base + 2, 8, stride=4)]
        odd_name = told[pl.ds(base + 3, 8, stride=4)]

        def whole(pair):
            return pair + share * pltpu.roll(pair, half, 1)

        value = jnp.where(left, whole(even_grad), pltpu.roll(whole(odd_grad), half, 1))
        ident = jnp.where(left, even_name, pltpu.roll(odd_name, half, 1)).astype(jnp.int32)
        upper = ident // DEPTH
        lower = ident - upper * DEPTH
        pieces = [piece.astype(jnp.float32) for piece in split3(value)]
        high_is = lax.broadcasted_iota(jnp.int32, (32, DEPTH), 0)
        low_is = lax.broadcasted_iota(jnp.int32, (DEPTH, DEPTH), 0)
        lhs, rhs = [], []
        for q in range(8):
            hot = high_is == jnp.broadcast_to(upper[q : q + 1], (32, DEPTH))
            lhs.append(
                jnp.concatenate(
                    [
                        jnp.where(hot, jnp.broadcast_to(piece[q : q + 1], (32, DEPTH)), 0.0)
                        for piece in pieces
                    ],
                    0,
                ).astype(jnp.bfloat16)
            )
            hot = low_is == jnp.broadcast_to(lower[q : q + 1], (DEPTH, DEPTH))
            rhs.append(jnp.where(hot, 1.0, 0.0).astype(jnp.bfloat16))
        return total + lax.dot_general(
            jnp.concatenate(lhs, 1),
            jnp.concatenate(rhs, 1),
            (((1,), (1,)), ((), ())),
            preferred_element_type=jnp.float32,
        )

    total = lax.fori_loop(0, rows // 16, one, jnp.zeros((96, DEPTH), jnp.float32), unroll=2)
    grad = (total[0:32] + total[32:64]) + total[64:96]
    new_first = BETA_ONE * first[...] + (1.0 - BETA_ONE) * grad
    new_second = BETA_TWO * second[...] + (1.0 - BETA_TWO) * grad * grad
    first_hat = new_first / (1.0 - BETA_ONE**ADAM_STEP)
    second_hat = new_second / (1.0 - BETA_TWO**ADAM_STEP)
    theta_new[...] = theta[...] - LEARN_RATE * first_hat / (jnp.sqrt(second_hat) + ADAM_EPS)
    first_new[...] = new_first
    second_new[...] = new_second
    for copy in copies:
        copy.wait()

    def combine(c):
        adjoint[c] = va[c] + share * vb[c]

    loop(26, combine)


def neighbour(value, axis, step):
    count = lax.axis_size(axis)
    return lax.ppermute(value, axis, [(i, (i + step) % count) for i in range(count)])


def forward_gx(value, k):
    count, group = lax.axis_size("gx"), lax.axis_size("st")
    pairs = []
    for g in range(count):
        for s in range(group):
            to = g + 1 if (s - k) % group >= HALO else g - 1
            pairs.append((g * group + s, (to % count) * group + s))
    return lax.ppermute(value, ("gx", "st"), pairs)


def after(value, *earlier):
    return lax.optimization_barrier((value, *earlier))[0]


def window(checkpoint, adjoint_in, solid_mask, tile_map, theta, first_moment, second_moment):
    vmem = pltpu.VMEM
    f32 = jnp.float32
    place = lax.axis_index("st").astype(jnp.int32).reshape(1)
    packed = call(
        pack_kernel, [(26, WIDE, DEPTH)] * 8, [vmem((26, 72, DEPTH), f32)], 12, 1, 2
    )(place, checkpoint[:, 0])

    planes = [packed[0]] + [None] * 7
    for k in (1, 7, 2, 6, 3, 5, 4):
        planes[k] = neighbour(packed[k], "st", k)
    halos = []
    for k in range(8):
        halos.append(forward_gx(planes[k], k))

    def both(value, axis):
        low, high = value
        low = neighbour(low, axis, 1)
        high = neighbour(high, axis, -1)
        return low, high

    plate = theta[after(tile_map, packed[0])]
    plate = jnp.broadcast_to(plate[:, :, None], (OWN, OWN, DEPTH))
    names = jnp.pad(tile_map.reshape(1, -1).astype(f32), ((0, 0), (0, DEPTH - OWN * OWN)))
    flags, names = lax.optimization_barrier((jnp.stack([solid_mask.astype(f32), plate]), names))
    low, high = both((flags[:, 4:8], flags[:, 0:4]), "gx")
    flags = jnp.concatenate([low, flags, high], 1)
    low, high = both((flags[:, :, 4:8], flags[:, :, 0:4]), "st")
    region = jnp.concatenate([low, flags, high], 2)
    table = call(table_kernel, [(WIDE, 20, WIDE, DEPTH)], mib=8)(region)[0]

    gl, gr = both((adjoint_in[:, 4:8], adjoint_in[:, 0:4]), "gx")
    tall = jnp.concatenate([gl, adjoint_in, gr], 1)
    slo, shi = both((tall[:, :, 4:8], tall[:, :, 0:4]), "st")

    big = (WIDE, 26, WIDE, DEPTH)
    mom, edge, edge_lo, edge_hi, heat = call(
        forward_kernel,
        [(3, WIDE, 4, WIDE, DEPTH), (OWN, 6, OWN, DEPTH), (OWN, 6, 4, DEPTH), (OWN, 6, 4, DEPTH), (1, DEPTH)],
        [vmem(big, f32), vmem(big, f32), vmem((WIDE, 4, WIDE, DEPTH), f32)],
        12,
        1,
        19,
    )(place, *planes, *halos, table, region)
    elo, ehi = both((edge_hi, edge_lo), "st")
    head, tail = call(merge_kernel, [(HALO, 6, WIDE, DEPTH)] * 2, mib=4)(elo, edge, ehi)
    el, er = both((tail, head), "gx")

    count = lax.axis_size("gx") * lax.axis_size("st")
    mine = (26, OWN, OWN, DEPTH)
    out_a, out_b, slots = call(
        backward_kernel,
        [mine, mine, (count, 2, DEPTH)],
        [vmem(big, f32)] * 4
        + [vmem((WIDE, 6, WIDE, DEPTH), f32), vmem((DEPTH, DEPTH), f32)]
        + [vmem(mine, f32)] * 2
        + [pltpu.SemaphoreType.DMA((2,))],
        24,
        out_specs=[pltpu.HBM, pltpu.HBM, pltpu.VMEM],
    )(adjoint_in, gl, gr, slo, shi, elo, edge, ehi, el, er, mom, table, region, names, heat)
    told = lax.all_to_all(slots, ("gx", "st"), 0, 0, tiled=True)

    scale = jnp.full((1,), 1.0 / (KAPPA * count * OWN * OWN), f32)
    tiles = (theta.shape[0] // DEPTH, DEPTH)
    theta_new, first_new, second_new, nusselt, adjoint = call(
        tile_kernel,
        [tiles] * 3 + [(1, 1), mine],
        [vmem(mine, f32)] * 2 + [pltpu.SemaphoreType.DMA((2,))],
        mib=12,
        in_specs=[pltpu.SMEM] + [pltpu.VMEM] * 4 + [pltpu.HBM] * 2,
        out_specs=[pltpu.VMEM] * 3 + [pltpu.SMEM, pltpu.VMEM],
    )(
        scale,
        told.reshape(2 * count, DEPTH),
        theta.reshape(tiles),
        first_moment.reshape(tiles),
        second_moment.reshape(tiles),
        out_a,
        out_b,
    )
    flat = theta.shape
    return (
        adjoint,
        theta_new.reshape(flat),
        first_new.reshape(flat),
        second_new.reshape(flat),
        nusselt.reshape(()),
    )


def solution(mesh):
    return jax.shard_map(
        window,
        mesh=mesh,
        in_specs=(
            P(None, ("gx", "st"), None, None),
            P(None, "gx", "st", None),
            P("gx", "st", None),
            P("gx", "st"),
            P(),
            P(),
            P(),
        ),
        out_specs=(P(None, "gx", "st", None), P(), P(), P(), P()),
        check_vma=False,
    )
```

```python
import jax
import jax.numpy as jnp
import numpy as np
from jax import lax
from jax.experimental import pallas as pl
from jax.experimental.pallas import tpu as pltpu
from jax.sharding import PartitionSpec as P


ADAM_STEP = 100

VELOCITY = np.array(
    [
        [0, 0, 0],
        [1, 0, 0],
        [-1, 0, 0],
        [0, 1, 0],
        [0, -1, 0],
        [0, 0, 1],
        [0, 0, -1],
        [1, 1, 0],
        [-1, -1, 0],
        [1, -1, 0],
        [-1, 1, 0],
        [1, 0, 1],
        [-1, 0, -1],
        [1, 0, -1],
        [-1, 0, 1],
        [0, 1, 1],
        [0, -1, -1],
        [0, 1, -1],
        [0, -1, 1],
        [0, 0, 0],
        [1, 0, 0],
        [-1, 0, 0],
        [0, 1, 0],
        [0, -1, 0],
        [0, 0, 1],
        [0, 0, -1],
    ],
    dtype=np.int32,
)
VEL = [tuple(int(v) for v in row) for row in VELOCITY]
OPP = [0, 2, 1, 4, 3, 6, 5, 8, 7, 10, 9, 12, 11, 14, 13, 16, 15, 18, 17, 19, 21, 20, 23, 22, 25, 24]
FLOW_PAIRS = [(i, i + 1) for i in range(1, 19, 2)]
HEAT_PAIRS = [(20, 21), (22, 23), (24, 25)]
INV_TAU = 1.25
KEEP = 1.0 - INV_TAU
LIFT = 0.8 * 0.001
MEAN_TEMP = 0.5
KAPPA = 0.075
RISING = 24
LEARN_RATE = 0.05
BETA_ONE = 0.9
BETA_TWO = 0.99
ADAM_EPS = 1e-08

HALO = 4
OWN = 8
WIDE = OWN + 2 * HALO
DEPTH = 128
INTERPRET = False


def weight(i):
    if i < 19:
        return 1.0 / 3.0 if i == 0 else (1.0 / 18.0 if i < 7 else 1.0 / 36.0)
    return 0.25 if i == 19 else 0.125


def call(kernel, outs, scratch=(), mib=8, scalars=0, inputs=None, out_specs=None, in_specs=None):
    extra = {}
    if in_specs:
        extra["in_specs"] = [pl.BlockSpec(memory_space=space) for space in in_specs]
    if scalars:
        extra["in_specs"] = [pl.BlockSpec(memory_space=pltpu.SMEM)] * scalars + [
            pl.BlockSpec(memory_space=pltpu.VMEM)
        ] * (inputs - scalars)
    if out_specs:
        extra["out_specs"] = [pl.BlockSpec(memory_space=space) for space in out_specs]
    return pl.pallas_call(
        kernel,
        out_shape=[jax.ShapeDtypeStruct(s, jnp.float32) for s in outs],
        scratch_shapes=list(scratch),
        compiler_params=pltpu.CompilerParams(vmem_limit_bytes=mib << 20),
        interpret=INTERPRET,
        **extra,
    )


class At:
    def __init__(self, index, offset):
        self.index, self.offset = index, offset

    def by(self, more):
        return self.index + (self.offset + more) if self.offset + more else self.index


def loop(count, fn):
    lax.fori_loop(0, count, lambda i, c: (fn(i), c)[1], 0)


def shifted(value, step_y, step_z):
    if step_y:
        value = pltpu.roll(value, step_y % value.shape[0], 0)
    if step_z:
        value = pltpu.roll(value, step_z % DEPTH, 1)
    return value


def lane_is(k, rows=WIDE):
    return lax.broadcasted_iota(jnp.int32, (rows, DEPTH), 1) == k


def table_of(i):
    if i >= 24:
        return i - 6
    if i >= 19:
        return i - 20
    return i - 1


def add_all(values):
    total = values[0]
    for value in values[1:]:
        total = total + value
    return total


def signed_sum(terms):
    total = None
    for sign, value in terms:
        if total is None:
            total = value if sign > 0 else -value
        else:
            total = total + value if sign > 0 else total - value
    return total


def moments(s):
    diff = {}
    parts = [s[0]]
    for i, j in FLOW_PAIRS:
        parts.append(s[i] + s[j])
        diff[i] = s[i] - s[j]
    density = add_all(parts)
    speed = []
    for axis in range(3):
        speed.append(signed_sum([(VEL[i][axis], diff[i]) for i, _ in FLOW_PAIRS if VEL[i][axis]]))
    temper = add_all([s[i] for i in range(19, 26)])
    return density, speed, temper


def collided(s, density, speed, temper):
    ux, uy, uz = speed
    vz = uz + LIFT * (temper - MEAN_TEMP)
    vel = (ux, uy, vz)
    base = density - 1.5 * (ux * ux + uy * uy + vz * vz)
    out = [None] * 26
    out[0] = KEEP * s[0] + (INV_TAU * weight(0)) * base
    for i, j in FLOW_PAIRS:
        proj = signed_sum([(VEL[i][a], vel[a]) for a in range(3) if VEL[i][a]])
        factor = INV_TAU * weight(i)
        even = factor * base + (4.5 * factor) * (proj * proj)
        odd = (3.0 * factor) * proj
        out[i] = KEEP * s[i] + (even + odd)
        out[j] = KEEP * s[j] + (even - odd)
    out[19] = KEEP * s[19] + (INV_TAU * weight(19)) * temper
    scaled = (INV_TAU * weight(20)) * temper
    for (i, j), u in zip(HEAT_PAIRS, (ux, uy, uz)):
        odd = scaled * (4.0 * u)
        out[i] = KEEP * s[i] + (scaled + odd)
        out[j] = KEEP * s[j] + (scaled - odd)
    return out


LINES = 26 * WIDE
FLAG_LINES = 2 * OWN * 4
PLANE_FLAGS = 2 * HALO * WIDE


def fill_tall(plane, tall):
    def fill(c):
        tall[c, 0:4] = plane[c, 60:64]
        tall[c, 4:68] = plane[c]
        tall[c, 68:72] = plane[c, 0:4]

    loop(26, fill)


def copy_slot(place, tall, k, out):
    base = pl.multiple_of(OWN * lax.rem(place[0] + k, 8), 8)

    def one(c):
        out[pl.ds(pl.multiple_of(WIDE * c, WIDE), WIDE)] = tall[c, pl.ds(base, WIDE)]

    loop(26, one)


def pack_kernel(place, plane, *refs):
    outs, tall = refs[:6], refs[6]
    fill_tall(plane, tall)
    for k, out in zip((0, 2, 3, 4, 5, 6), outs):
        copy_slot(place, tall, k, out)


def pack_flags_kernel(place, plane, flags, up, down, tall):
    fill_tall(plane, tall)
    copy_slot(place, tall, 1, up)
    copy_slot(place, tall, 7, down)
    for f in range(2):
        for x in range(OWN):
            at = LINES + 4 * (OWN * f + x)
            up[at : at + 4] = flags[f, x, 4:8]
            down[at : at + 4] = flags[f, x, 0:4]


def tall_flags(flags, low, high, f, x):
    at = LINES + 4 * (OWN * f + x)
    return ((0, 4, low[at : at + 4]), (4, 12, flags[f, x]), (12, 16, high[at : at + 4]))


def route_kernel(place, pairs, refs, plus, minus):
    for q, k in enumerate(pairs):
        n = lax.rem(place[0] + (8 - k), 8)
        one, two = refs[2 * q], refs[2 * q + 1]

        def move(first, second, q=q):
            def step(c):
                there = pl.ds(pl.multiple_of(32 * c, 32), 32)
                to = pl.ds(pl.multiple_of(32 * c + LINES * q, 32), 32)
                plus[to] = first[there]
                minus[to] = second[there]

            loop(LINES // 32, step)

        @pl.when(n >= HALO)
        def _(move=move, one=one, two=two):
            move(one, two)

        @pl.when(n < HALO)
        def _(move=move, one=one, two=two):
            move(two, one)


FIRST, SECOND = (1, 3), (0, 2)


def route_first_kernel(place, a, b, c, d, flags, plus, minus):
    route_kernel(place, FIRST, (a, b, c, d), plus, minus)
    low, high = a, d
    for f in range(2):
        for n in range(HALO):
            at = 2 * LINES + WIDE * (HALO * f + n)
            for lo, hi, value in tall_flags(flags, low, high, f, n + HALO):
                plus[at + lo : at + hi] = value
            for lo, hi, value in tall_flags(flags, low, high, f, n):
                minus[at + lo : at + hi] = value


def route_second_kernel(place, a, b, c, d, plus, minus):
    route_kernel(place, SECOND, (a, b, c, d), plus, minus)


def table_kernel(low, high, flags, from_left, from_right, region, table):
    for f in range(2):
        for x in range(OWN):
            for lo, hi, value in tall_flags(flags, low, high, f, x):
                region[f, x + HALO, lo:hi] = value
        for n in range(HALO):
            at = 2 * LINES + WIDE * (HALO * f + n)
            region[f, n] = from_left[at : at + WIDE]
            region[f, n + HALO + OWN] = from_right[at : at + WIDE]
    first = lane_is(0)
    last = lane_is(DEPTH - 1)

    def one(n):
        at = At(n, 1)
        x = at.by(0)
        for i in range(1, 19):
            cx, cy, cz = VEL[i]
            value = shifted(region[0, at.by(-cx)], cy, cz)
            if cz:
                edge = first if cz > 0 else last
                if i in (5, 6):
                    table[x, table_of(i + 19)] = jnp.where(edge, -1.0, value)
                value = jnp.where(edge, 1.0, value)
            table[x, table_of(i)] = value

    loop(WIDE - 2, one)


def streamed(p, table, at):
    x = at.by(0)
    s = []
    for i in range(26):
        if i in (0, 19):
            s.append(p[x, i])
            continue
        cx, cy, cz = VEL[i]
        moved = shifted(p[at.by(-cx), i], cy, cz)
        t = table[x, table_of(i)]
        back = p[x, OPP[i]]
        if i >= 24:
            back = t * back
        s.append(jnp.where(t == 0.0, moved, back))
    return s


def forward_kernel(place, *refs):
    planes, halos = refs[:8], refs[8:12]
    table, region, mom, edge, edge_lo, edge_hi, heat, pa, pb, mom3 = refs[12:]
    first = lane_is(0)

    def start(src, x, off=0):
        s = [src[off + WIDE * i : off + WIDE * (i + 1)] for i in range(26)]
        density, speed, temper = moments(s)
        for a, value in enumerate((*speed, temper)):
            mom[0, x, a] = value
        for i, value in enumerate(collided(s, density, speed, temper)):
            pa[x, i] = value

    for k in range(8):
        n = lax.rem(place[0] + (8 - k), 8)
        start(planes[k], n + HALO)
    for group, pairs in enumerate((FIRST, SECOND)):
        for q, k in enumerate(pairs):
            n = lax.rem(place[0] + (8 - k), HALO)
            start(halos[2 * group], n, LINES * q)
            start(halos[2 * group + 1], n + OWN + HALO, LINES * q)

    def arrive(p, at):
        s = streamed(p, table, at)
        s[RISING] = s[RISING] + jnp.where(first, 0.25 * region[1, at.by(0)], 0.0)
        return s

    src, dst = pa, pb
    for k in range(1, 4):

        def one(n, k=k, src=src, dst=dst):
            at = At(n, k)
            x = at.by(0)
            s = arrive(src, at)
            density, speed, temper = moments(s)
            for a, value in enumerate((*speed, temper)):
                if k < 3:
                    mom[k, x, a] = value
                else:
                    mom3[x, a] = value
            for i, value in enumerate(collided(s, density, speed, temper)):
                dst[x, i] = value

        loop(WIDE - 2 * k, one)
        src, dst = dst, src

    def last(n, total):
        at = At(n, HALO)
        x = at.by(0)
        s = arrive(src, at)
        _, speed, temper = moments(s)
        values = [mom3[x, a] for a in range(4)] + [speed[2], temper]
        for a, value in enumerate(values):
            edge[n, a] = value[4:12]
            edge_lo[n, a] = value[4:8]
            edge_hi[n, a] = value[8:12]
        flux = (1.0 - region[0, x]) * speed[2] * temper
        return total + flux[4:12]

    total = lax.fori_loop(0, OWN, last, jnp.zeros((OWN, DEPTH), jnp.float32))
    heat[...] = jnp.broadcast_to(jnp.sum(total), heat.shape)


def adjoint_cell(lam, table, at, fluids, vel, temper):
    x = at.by(0)
    fluid, fluid_up, fluid_down = fluids
    ux, uy, uz = vel
    vz = uz + LIFT * (temper - MEAN_TEMP)
    v = (ux, uy, vz)

    def mu_of(j):
        cx, cy, cz = VEL[j]
        if j in (0, 19):
            return lam[x, j]
        moved = shifted(lam[at.by(cx), j], -cy, -cz)
        keep = fluid if cz == 0 else (fluid_up if cz > 0 else fluid_down)
        return keep * moved + table[x, table_of(OPP[j])] * lam[x, OPP[j]]

    mu = [mu_of(j) for j in range(26)]
    axis_sum = add_all([mu[i] + mu[j] for i, j in FLOW_PAIRS[:3]])
    pair_sum = {i: mu[i] + mu[j] for i, j in FLOW_PAIRS}
    pair_diff = {i: mu[i] - mu[j] for i, j in FLOW_PAIRS}
    wa, wd = weight(1), weight(7)
    diag = add_all([pair_sum[i] for i, _ in FLOW_PAIRS[3:]])
    zeroth = weight(0) * mu[0] + wa * axis_sum + wd * diag

    def first(a):
        axis = 1 + 2 * a
        rest = signed_sum([(VEL[i][a], pair_diff[i]) for i, _ in FLOW_PAIRS[3:] if VEL[i][a]])
        return wa * pair_diff[axis] + wd * rest

    def second(a, b):
        if a == b:
            rest = add_all([pair_sum[i] for i, _ in FLOW_PAIRS[3:] if VEL[i][a]])
            return wa * pair_sum[1 + 2 * a] + wd * rest
        return wd * signed_sum(
            [(VEL[i][a] * VEL[i][b], pair_sum[i]) for i, _ in FLOW_PAIRS[3:] if VEL[i][a] * VEL[i][b]]
        )

    m2 = {(a, b): second(a, b) for a in range(3) for b in range(a, 3)}
    force = []
    for a in range(3):
        bent = add_all([m2[min(a, b), max(a, b)] * v[b] for b in range(3)])
        force.append(3.0 * first(a) + 9.0 * bent - 3.0 * (v[a] * zeroth))
    heat_diff = [mu[i] - mu[j] for i, j in HEAT_PAIRS]
    heat_even = weight(19) * mu[19] + weight(20) * add_all([mu[i] + mu[j] for i, j in HEAT_PAIRS])
    wh = 4.0 * weight(20)
    heat_odd = add_all([heat_diff[a] * (wh * u) for a, u in enumerate((ux, uy, uz))])
    to_heat = INV_TAU * (LIFT * force[2] + heat_even + heat_odd)
    scaled = wh * temper
    pull = [INV_TAU * (force[a] + scaled * heat_diff[a]) for a in range(3)]
    base = INV_TAU * zeroth
    out = [None] * 26
    out[0] = KEEP * mu[0] + base
    for i, j in FLOW_PAIRS:
        proj = signed_sum([(VEL[i][a], pull[a]) for a in range(3) if VEL[i][a]])
        out[i] = KEEP * mu[i] + (base + proj)
        out[j] = KEEP * mu[j] + (base - proj)
    for i in range(19, 26):
        out[i] = KEEP * mu[i] + to_heat
    return out


def merge_kernel(lo, mid, hi, head, tail):
    for n in range(HALO):
        for out, x in ((head, n), (tail, n + HALO)):
            for a in range(6):
                out[n, a, 0:4] = lo[x, a]
                out[n, a, 4:12] = mid[x, a]
                out[n, a, 12:16] = hi[x, a]


def adjoint_planes(k, state_of, bufs, table, region, put):
    first = lane_is(0)
    last = lane_is(DEPTH - 1)

    def one(n):
        at = At(n, HALO - k)
        x = at.by(0)
        fluid = 1.0 - region[0, x]
        fluids = (fluid, jnp.where(last, 0.0, fluid), jnp.where(first, 0.0, fluid))
        state = [state_of(x, a) for a in range(4)]
        for chain, src in enumerate(bufs):
            lam = adjoint_cell(src, table, at, fluids, state[:3], state[3])
            for i in range(26):
                put(chain, n, x, i, lam[i])

    loop(OWN + 2 * k, one)


def backward_kernel(*refs):
    own, gl, gr, slo, shi, elo, emid, ehi, el, er, mom, table, region, names, heat = refs[:15]
    out_a, out_b, slots, la0, la1, lb0, lb1, late, sums, last_a, last_b, sems = refs[15:]

    def gather(src, count, off):
        def one(x):
            for i in range(26):
                la0[x + off, i, 0:4] = slo[i, x + off]
                la0[x + off, i, 4:12] = src[i, x]
                la0[x + off, i, 12:16] = shi[i, x + off]

        loop(count, one)

    gather(gl, HALO, 0)
    gather(own, OWN, HALO)
    gather(gr, HALO, HALO + OWN)

    def settle(x):
        for a in range(6):
            late[x + HALO, a, 0:4] = elo[x, a]
            late[x + HALO, a, 4:12] = emid[x, a]
            late[x + HALO, a, 12:16] = ehi[x, a]

    loop(OWN, settle)

    def flank(x):
        for a in range(6):
            late[x, a] = el[x, a]
            late[x + HALO + OWN, a] = er[x, a]

    loop(HALO, flank)

    def seed(x):
        fluid = 1.0 - region[0, x]
        up = fluid * late[x, 5]
        zero = jnp.zeros_like(up)
        heat = fluid * late[x, 4]
        for i in range(26):
            cz = VEL[i][2]
            lb0[x, i] = heat if i >= 19 else (zero if cz == 0 else (up if cz > 0 else -up))

    loop(WIDE, seed)

    def collect(chain, lam, fresh):
        for n in range(OWN):
            value = lam[n + HALO, RISING][4:12]
            spot = pl.ds(OWN * OWN * chain + OWN * n, OWN)
            sums[spot] = value if fresh else sums[spot] + value

    bufs = [(la0, la1), (lb0, lb1)]
    for k in (3, 2, 1, 0):
        for chain, (src, _) in enumerate(bufs):
            collect(chain, src, k == 3)

        def put(chain, n, x, i, value, k=k, dsts=(bufs[0][1], bufs[1][1])):
            if k == 0:
                (last_a, last_b)[chain][i, n] = value[4:12]
            else:
                dsts[chain][x, i] = value

        def state_of(x, a, k=k):
            return late[x, a] if k == 3 else mom[k, x, a]

        adjoint_planes(k, state_of, [src for src, _ in bufs], table, region, put)
        bufs = [(dst, src) for src, dst in bufs]
    copies = [
        pltpu.make_async_copy(last_a, out_a, sems.at[0]),
        pltpu.make_async_copy(last_b, out_b, sems.at[1]),
    ]
    for copy in copies:
        copy.start()

    line = 0.25 * jnp.transpose(sums[...])[0:1]
    lane = lax.broadcasted_iota(jnp.int32, (1, DEPTH), 1)
    pair = jnp.concatenate([line, jnp.where(lane < OWN * OWN, names[...], heat[...])], 0)
    count = slots.shape[0]

    def spread(n):
        for q in range(8):
            slots[8 * n + q] = pair

    loop(count // 8, spread)
    for copy in copies:
        copy.wait()


def split3(value):
    high = value.astype(jnp.bfloat16)
    rest = value - high.astype(jnp.float32)
    mid = rest.astype(jnp.bfloat16)
    low = (rest - mid.astype(jnp.float32)).astype(jnp.bfloat16)
    return high, mid, low


def tile_kernel(
    scale, told, theta, first, second, part_a, part_b, theta_new, first_new, second_new, nusselt, adjoint, va, vb, sems
):
    copies = [
        pltpu.make_async_copy(part_a, va, sems.at[0]),
        pltpu.make_async_copy(part_b, vb, sems.at[1]),
    ]
    for copy in copies:
        copy.start()
    rows = told.shape[0] // 2
    half = DEPTH // 2
    lane = lax.broadcasted_iota(jnp.int32, (8, DEPTH), 1)
    left = lane < half

    def flux(r, total):
        return total + told[pl.ds(pl.multiple_of(8 * r, 8), 8)]

    total = lax.fori_loop(0, rows // 4, flux, jnp.zeros((8, DEPTH), jnp.float32), unroll=8)
    odd = lax.rem(lax.broadcasted_iota(jnp.int32, (8, DEPTH), 0), 2) == 1
    share = jnp.sum(jnp.where(odd & (lane == half), total, 0.0)) * scale[0]
    nusselt[0, 0] = 1.0 + share

    def one(r, total):
        base = pl.multiple_of(32 * r, 32)
        even_grad = told[pl.ds(base, 8, stride=4)]
        even_name = told[pl.ds(base + 1, 8, stride=4)]
        odd_grad = told[pl.ds(base + 2, 8, stride=4)]
        odd_name = told[pl.ds(base + 3, 8, stride=4)]

        def whole(pair):
            return pair + share * pltpu.roll(pair, half, 1)

        value = jnp.where(left, whole(even_grad), pltpu.roll(whole(odd_grad), half, 1))
        ident = jnp.where(left, even_name, pltpu.roll(odd_name, half, 1)).astype(jnp.int32)
        upper = ident // DEPTH
        lower = ident - upper * DEPTH
        pieces = [piece.astype(jnp.float32) for piece in split3(value)]
        high_is = lax.broadcasted_iota(jnp.int32, (32, DEPTH), 0)
        low_is = lax.broadcasted_iota(jnp.int32, (DEPTH, DEPTH), 0)
        lhs, rhs = [], []
        for q in range(8):
            hot = high_is == jnp.broadcast_to(upper[q : q + 1], (32, DEPTH))
            lhs.append(
                jnp.concatenate(
                    [
                        jnp.where(hot, jnp.broadcast_to(piece[q : q + 1], (32, DEPTH)), 0.0)
                        for piece in pieces
                    ],
                    0,
                ).astype(jnp.bfloat16)
            )
            hot = low_is == jnp.broadcast_to(lower[q : q + 1], (DEPTH, DEPTH))
            rhs.append(jnp.where(hot, 1.0, 0.0).astype(jnp.bfloat16))
        return total + lax.dot_general(
            jnp.concatenate(lhs, 1),
            jnp.concatenate(rhs, 1),
            (((1,), (1,)), ((), ())),
            preferred_element_type=jnp.float32,
        )

    total = lax.fori_loop(0, rows // 16, one, jnp.zeros((96, DEPTH), jnp.float32), unroll=2)
    grad = (total[0:32] + total[32:64]) + total[64:96]
    new_first = BETA_ONE * first[...] + (1.0 - BETA_ONE) * grad
    new_second = BETA_TWO * second[...] + (1.0 - BETA_TWO) * grad * grad
    first_hat = new_first / (1.0 - BETA_ONE**ADAM_STEP)
    second_hat = new_second / (1.0 - BETA_TWO**ADAM_STEP)
    theta_new[...] = theta[...] - LEARN_RATE * first_hat / (jnp.sqrt(second_hat) + ADAM_EPS)
    first_new[...] = new_first
    second_new[...] = new_second
    for copy in copies:
        copy.wait()

    def combine(c):
        adjoint[c] = va[c] + share * vb[c]

    loop(26, combine)


def neighbour(value, axis, step):
    count = lax.axis_size(axis)
    return lax.ppermute(value, axis, [(i, (i + step) % count) for i in range(count)])


def after(value, *earlier):
    return lax.optimization_barrier((value, *earlier))[0]


def window(checkpoint, adjoint_in, solid_mask, tile_map, theta, first_moment, second_moment):
    vmem = pltpu.VMEM
    f32 = jnp.float32
    place = lax.axis_index("st").astype(jnp.int32).reshape(1)
    smem, on_chip = [pltpu.SMEM], pltpu.VMEM
    plane = checkpoint[:, 0]
    tall = vmem((26, 72, DEPTH), f32)
    slots = call(pack_kernel, [(LINES, DEPTH)] * 6, [tall], 12, in_specs=smem + [on_chip])(place, plane)
    packed = dict(zip((0, 2, 3, 4, 5, 6), slots))

    plate = theta[after(tile_map, packed[0])]
    plate = jnp.broadcast_to(plate[:, :, None], (OWN, OWN, DEPTH))
    names = jnp.pad(tile_map.reshape(1, -1).astype(f32), ((0, 0), (0, DEPTH - OWN * OWN)))
    flags, names = lax.optimization_barrier((jnp.stack([solid_mask.astype(f32), plate]), names))
    packed[1], packed[7] = call(
        pack_flags_kernel, [(LINES + FLAG_LINES, DEPTH)] * 2, [tall], 12, in_specs=smem + [on_chip] * 2
    )(place, plane, flags)

    planes = [packed[0]] + [None] * 7
    for k in (5, 3, 1, 7, 2, 6, 4):
        planes[k] = neighbour(packed[k], "st", k)

    def both(value, axis):
        low, high = value
        low = neighbour(low, axis, 1)
        high = neighbour(high, axis, -1)
        return low, high

    halos = []
    lines = 2 * LINES + PLANE_FLAGS
    sent = call(route_first_kernel, [(lines, DEPTH)] * 2, (), 8, in_specs=smem + [on_chip] * 5)(
        place, planes[1], planes[5], planes[3], planes[7], flags
    )
    halos += both(sent, "gx")
    region, table = call(table_kernel, [(2, WIDE, WIDE, DEPTH), (WIDE, 20, WIDE, DEPTH)], mib=8)(
        planes[1], planes[7], flags, *halos
    )
    sent = call(route_second_kernel, [(2 * LINES, DEPTH)] * 2, (), 8, in_specs=smem + [on_chip] * 4)(
        place, planes[0], planes[4], planes[2], planes[6]
    )
    halos += both(sent, "gx")

    gl, gr = both((adjoint_in[:, 4:8], adjoint_in[:, 0:4]), "gx")
    tall = jnp.concatenate([gl, adjoint_in, gr], 1)
    slo, shi = both((tall[:, :, 4:8], tall[:, :, 0:4]), "st")

    big = (WIDE, 26, WIDE, DEPTH)
    mom, edge, edge_lo, edge_hi, heat = call(
        forward_kernel,
        [(3, WIDE, 4, WIDE, DEPTH), (OWN, 6, OWN, DEPTH), (OWN, 6, 4, DEPTH), (OWN, 6, 4, DEPTH), (1, DEPTH)],
        [vmem(big, f32), vmem(big, f32), vmem((WIDE, 4, WIDE, DEPTH), f32)],
        12,
        1,
        15,
    )(place, *planes, *halos, table, region)
    elo, ehi = both((edge_hi, edge_lo), "st")
    head, tail = call(merge_kernel, [(HALO, 6, WIDE, DEPTH)] * 2, mib=4)(elo, edge, ehi)
    el, er = both((tail, head), "gx")

    count = lax.axis_size("gx") * lax.axis_size("st")
    mine = (26, OWN, OWN, DEPTH)
    out_a, out_b, slots = call(
        backward_kernel,
        [mine, mine, (count, 2, DEPTH)],
        [vmem(big, f32)] * 4
        + [vmem((WIDE, 6, WIDE, DEPTH), f32), vmem((DEPTH, DEPTH), f32)]
        + [vmem(mine, f32)] * 2
        + [pltpu.SemaphoreType.DMA((2,))],
        24,
        out_specs=[pltpu.HBM, pltpu.HBM, pltpu.VMEM],
    )(adjoint_in, gl, gr, slo, shi, elo, edge, ehi, el, er, mom, table, region, names, heat)
    told = lax.all_to_all(slots, ("gx", "st"), 0, 0, tiled=True)

    scale = jnp.full((1,), 1.0 / (KAPPA * count * OWN * OWN), f32)
    tiles = (theta.shape[0] // DEPTH, DEPTH)
    theta_new, first_new, second_new, nusselt, adjoint = call(
        tile_kernel,
        [tiles] * 3 + [(1, 1), mine],
        [vmem(mine, f32)] * 2 + [pltpu.SemaphoreType.DMA((2,))],
        mib=12,
        in_specs=[pltpu.SMEM] + [pltpu.VMEM] * 4 + [pltpu.HBM] * 2,
        out_specs=[pltpu.VMEM] * 3 + [pltpu.SMEM, pltpu.VMEM],
    )(
        scale,
        told.reshape(2 * count, DEPTH),
        theta.reshape(tiles),
        first_moment.reshape(tiles),
        second_moment.reshape(tiles),
        out_a,
        out_b,
    )
    flat = theta.shape
    return (
        adjoint,
        theta_new.reshape(flat),
        first_new.reshape(flat),
        second_new.reshape(flat),
        nusselt.reshape(()),
    )


def solution(mesh):
    return jax.shard_map(
        window,
        mesh=mesh,
        in_specs=(
            P(None, ("gx", "st"), None, None),
            P(None, "gx", "st", None),
            P("gx", "st", None),
            P("gx", "st"),
            P(),
            P(),
            P(),
        ),
        out_specs=(P(None, "gx", "st", None), P(), P(), P(), P()),
        check_vma=False,
    )
```

```python
import jax
import jax.numpy as jnp
import numpy as np
from jax import lax
from jax.experimental import pallas as pl
from jax.experimental.pallas import tpu as pltpu
from jax.sharding import PartitionSpec as P


ADAM_STEP = 100

VELOCITY = np.array(
    [
        [0, 0, 0],
        [1, 0, 0],
        [-1, 0, 0],
        [0, 1, 0],
        [0, -1, 0],
        [0, 0, 1],
        [0, 0, -1],
        [1, 1, 0],
        [-1, -1, 0],
        [1, -1, 0],
        [-1, 1, 0],
        [1, 0, 1],
        [-1, 0, -1],
        [1, 0, -1],
        [-1, 0, 1],
        [0, 1, 1],
        [0, -1, -1],
        [0, 1, -1],
        [0, -1, 1],
        [0, 0, 0],
        [1, 0, 0],
        [-1, 0, 0],
        [0, 1, 0],
        [0, -1, 0],
        [0, 0, 1],
        [0, 0, -1],
    ],
    dtype=np.int32,
)
VEL = [tuple(int(v) for v in row) for row in VELOCITY]
OPP = [0, 2, 1, 4, 3, 6, 5, 8, 7, 10, 9, 12, 11, 14, 13, 16, 15, 18, 17, 19, 21, 20, 23, 22, 25, 24]
FLOW_PAIRS = [(i, i + 1) for i in range(1, 19, 2)]
HEAT_PAIRS = [(20, 21), (22, 23), (24, 25)]
INV_TAU = 1.25
KEEP = 1.0 - INV_TAU
LIFT = 0.8 * 0.001
MEAN_TEMP = 0.5
KAPPA = 0.075
RISING = 24
LEARN_RATE = 0.05
BETA_ONE = 0.9
BETA_TWO = 0.99
ADAM_EPS = 1e-08

HALO = 4
OWN = 8
WIDE = OWN + 2 * HALO
DEPTH = 128
INTERPRET = False


def weight(i):
    if i < 19:
        return 1.0 / 3.0 if i == 0 else (1.0 / 18.0 if i < 7 else 1.0 / 36.0)
    return 0.25 if i == 19 else 0.125


def call(kernel, outs, scratch=(), mib=8, scalars=0, inputs=None, out_specs=None, in_specs=None):
    extra = {}
    if in_specs:
        extra["in_specs"] = [pl.BlockSpec(memory_space=space) for space in in_specs]
    if scalars:
        extra["in_specs"] = [pl.BlockSpec(memory_space=pltpu.SMEM)] * scalars + [
            pl.BlockSpec(memory_space=pltpu.VMEM)
        ] * (inputs - scalars)
    if out_specs:
        extra["out_specs"] = [pl.BlockSpec(memory_space=space) for space in out_specs]
    return pl.pallas_call(
        kernel,
        out_shape=[jax.ShapeDtypeStruct(s, jnp.float32) for s in outs],
        scratch_shapes=list(scratch),
        compiler_params=pltpu.CompilerParams(vmem_limit_bytes=mib << 20),
        interpret=INTERPRET,
        **extra,
    )


class At:
    def __init__(self, index, offset):
        self.index, self.offset = index, offset

    def by(self, more):
        return self.index + (self.offset + more) if self.offset + more else self.index


def loop(count, fn):
    lax.fori_loop(0, count, lambda i, c: (fn(i), c)[1], 0)


def shifted(value, step_y, step_z):
    if step_y:
        value = pltpu.roll(value, step_y % value.shape[0], 0)
    if step_z:
        value = pltpu.roll(value, step_z % DEPTH, 1)
    return value


def lane_is(k, rows=WIDE):
    return lax.broadcasted_iota(jnp.int32, (rows, DEPTH), 1) == k


def table_of(i):
    if i >= 24:
        return i - 6
    if i >= 19:
        return i - 20
    return i - 1


def add_all(values):
    total = values[0]
    for value in values[1:]:
        total = total + value
    return total


def signed_sum(terms):
    total = None
    for sign, value in terms:
        if total is None:
            total = value if sign > 0 else -value
        else:
            total = total + value if sign > 0 else total - value
    return total


def moments(s):
    diff = {}
    parts = [s[0]]
    for i, j in FLOW_PAIRS:
        parts.append(s[i] + s[j])
        diff[i] = s[i] - s[j]
    density = add_all(parts)
    speed = []
    for axis in range(3):
        speed.append(signed_sum([(VEL[i][axis], diff[i]) for i, _ in FLOW_PAIRS if VEL[i][axis]]))
    temper = add_all([s[i] for i in range(19, 26)])
    return density, speed, temper


def collided(s, density, speed, temper):
    ux, uy, uz = speed
    vz = uz + LIFT * (temper - MEAN_TEMP)
    vel = (ux, uy, vz)
    base = density - 1.5 * (ux * ux + uy * uy + vz * vz)
    out = [None] * 26
    out[0] = KEEP * s[0] + (INV_TAU * weight(0)) * base
    for i, j in FLOW_PAIRS:
        proj = signed_sum([(VEL[i][a], vel[a]) for a in range(3) if VEL[i][a]])
        factor = INV_TAU * weight(i)
        even = factor * base + (4.5 * factor) * (proj * proj)
        odd = (3.0 * factor) * proj
        out[i] = KEEP * s[i] + (even + odd)
        out[j] = KEEP * s[j] + (even - odd)
    out[19] = KEEP * s[19] + (INV_TAU * weight(19)) * temper
    scaled = (INV_TAU * weight(20)) * temper
    for (i, j), u in zip(HEAT_PAIRS, (ux, uy, uz)):
        odd = scaled * (4.0 * u)
        out[i] = KEEP * s[i] + (scaled + odd)
        out[j] = KEEP * s[j] + (scaled - odd)
    return out


LINES = 26 * WIDE
FLAG_LINES = 2 * OWN * 4
PLANE_FLAGS = 2 * HALO * WIDE


def fill_tall(plane, tall):
    def fill(c):
        tall[c, 0:4] = plane[c, 60:64]
        tall[c, 4:68] = plane[c]
        tall[c, 68:72] = plane[c, 0:4]

    loop(26, fill)


def copy_slot(place, tall, k, out):
    base = pl.multiple_of(OWN * lax.rem(place[0] + k, 8), 8)

    def one(c):
        out[pl.ds(pl.multiple_of(WIDE * c, WIDE), WIDE)] = tall[c, pl.ds(base, WIDE)]

    loop(26, one)


def pack_kernel(place, plane, *refs):
    outs, tall = refs[:6], refs[6]
    fill_tall(plane, tall)
    for k, out in zip((0, 2, 3, 4, 5, 6), outs):
        copy_slot(place, tall, k, out)


def pack_flags_kernel(place, plane, flags, up, down, tall):
    fill_tall(plane, tall)
    copy_slot(place, tall, 1, up)
    copy_slot(place, tall, 7, down)
    for f in range(2):
        for x in range(OWN):
            at = LINES + 4 * (OWN * f + x)
            up[at : at + 4] = flags[f, x, 4:8]
            down[at : at + 4] = flags[f, x, 0:4]


def tall_flags(flags, low, high, f, x):
    at = LINES + 4 * (OWN * f + x)
    return ((0, 4, low[at : at + 4]), (4, 12, flags[f, x]), (12, 16, high[at : at + 4]))


def route_kernel(place, pairs, refs, plus, minus):
    for q, k in enumerate(pairs):
        n = lax.rem(place[0] + (8 - k), 8)
        one, two = refs[2 * q], refs[2 * q + 1]

        def move(first, second, q=q):
            def step(c):
                there = pl.ds(pl.multiple_of(32 * c, 32), 32)
                to = pl.ds(pl.multiple_of(32 * c + LINES * q, 32), 32)
                plus[to] = first[there]
                minus[to] = second[there]

            loop(LINES // 32, step)

        @pl.when(n >= HALO)
        def _(move=move, one=one, two=two):
            move(one, two)

        @pl.when(n < HALO)
        def _(move=move, one=one, two=two):
            move(two, one)


FIRST, SECOND = (1, 3), (0, 2)


def route_first_kernel(place, a, b, c, d, flags, plus, minus):
    route_kernel(place, FIRST, (a, b, c, d), plus, minus)
    low, high = a, d
    for f in range(2):
        for n in range(HALO):
            at = 2 * LINES + WIDE * (HALO * f + n)
            for lo, hi, value in tall_flags(flags, low, high, f, n + HALO):
                plus[at + lo : at + hi] = value
            for lo, hi, value in tall_flags(flags, low, high, f, n):
                minus[at + lo : at + hi] = value


def route_second_kernel(place, a, b, c, d, plus, minus):
    route_kernel(place, SECOND, (a, b, c, d), plus, minus)


def table_kernel(low, high, flags, from_left, from_right, region, table):
    for f in range(2):
        for x in range(OWN):
            for lo, hi, value in tall_flags(flags, low, high, f, x):
                region[f, x + HALO, lo:hi] = value
        for n in range(HALO):
            at = 2 * LINES + WIDE * (HALO * f + n)
            region[f, n] = from_left[at : at + WIDE]
            region[f, n + HALO + OWN] = from_right[at : at + WIDE]
    first = lane_is(0)
    last = lane_is(DEPTH - 1)

    def one(n):
        at = At(n, 1)
        x = at.by(0)
        for i in range(1, 19):
            cx, cy, cz = VEL[i]
            value = shifted(region[0, at.by(-cx)], cy, cz)
            if cz:
                edge = first if cz > 0 else last
                if i in (5, 6):
                    table[x, table_of(i + 19)] = jnp.where(edge, -1.0, value)
                value = jnp.where(edge, 1.0, value)
            table[x, table_of(i)] = value

    loop(WIDE - 2, one)


def streamed(p, table, at):
    x = at.by(0)
    s = []
    for i in range(26):
        if i in (0, 19):
            s.append(p[x, i])
            continue
        cx, cy, cz = VEL[i]
        moved = shifted(p[at.by(-cx), i], cy, cz)
        t = table[x, table_of(i)]
        back = p[x, OPP[i]]
        if i >= 24:
            back = t * back
        s.append(jnp.where(t == 0.0, moved, back))
    return s


def forward_kernel(place, *refs):
    planes, halos = refs[:8], refs[8:12]
    table, region, mom, edge, edge_lo, edge_hi, heat, pa, pb, mom3 = refs[12:]
    first = lane_is(0)

    def start(src, x, off=0):
        s = [src[off + WIDE * i : off + WIDE * (i + 1)] for i in range(26)]
        density, speed, temper = moments(s)
        for a, value in enumerate((*speed, temper)):
            mom[0, x, a] = value
        for i, value in enumerate(collided(s, density, speed, temper)):
            pa[x, i] = value

    for k in range(8):
        n = lax.rem(place[0] + (8 - k), 8)
        start(planes[k], n + HALO)
    for group, pairs in enumerate((FIRST, SECOND)):
        for q, k in enumerate(pairs):
            n = lax.rem(place[0] + (8 - k), HALO)
            start(halos[2 * group], n, LINES * q)
            start(halos[2 * group + 1], n + OWN + HALO, LINES * q)

    def arrive(p, at):
        s = streamed(p, table, at)
        s[RISING] = s[RISING] + jnp.where(first, 0.25 * region[1, at.by(0)], 0.0)
        return s

    src, dst = pa, pb
    for k in range(1, 4):

        def one(n, k=k, src=src, dst=dst):
            at = At(n, k)
            x = at.by(0)
            s = arrive(src, at)
            density, speed, temper = moments(s)
            for a, value in enumerate((*speed, temper)):
                if k < 3:
                    mom[k, x, a] = value
                else:
                    mom3[x, a] = value
            for i, value in enumerate(collided(s, density, speed, temper)):
                dst[x, i] = value

        loop(WIDE - 2 * k, one)
        src, dst = dst, src

    def last(n, total):
        at = At(n, HALO)
        x = at.by(0)
        s = arrive(src, at)
        _, speed, temper = moments(s)
        values = [mom3[x, a] for a in range(4)] + [speed[2], temper]
        for a, value in enumerate(values):
            edge[n, a] = value[4:12]
            edge_lo[n, a] = value[4:8]
            edge_hi[n, a] = value[8:12]
        flux = (1.0 - region[0, x]) * speed[2] * temper
        return total + flux[4:12]

    total = lax.fori_loop(0, OWN, last, jnp.zeros((OWN, DEPTH), jnp.float32))
    heat[...] = jnp.broadcast_to(jnp.sum(total), heat.shape)


def adjoint_cell(lam, table, at, fluids, vel, temper):
    x = at.by(0)
    fluid, fluid_up, fluid_down = fluids
    ux, uy, uz = vel
    vz = uz + LIFT * (temper - MEAN_TEMP)
    v = (ux, uy, vz)

    def mu_of(j):
        cx, cy, cz = VEL[j]
        if j in (0, 19):
            return lam[x, j]
        moved = shifted(lam[at.by(cx), j], -cy, -cz)
        keep = fluid if cz == 0 else (fluid_up if cz > 0 else fluid_down)
        return keep * moved + table[x, table_of(OPP[j])] * lam[x, OPP[j]]

    mu = [mu_of(j) for j in range(26)]
    axis_sum = add_all([mu[i] + mu[j] for i, j in FLOW_PAIRS[:3]])
    pair_sum = {i: mu[i] + mu[j] for i, j in FLOW_PAIRS}
    pair_diff = {i: mu[i] - mu[j] for i, j in FLOW_PAIRS}
    wa, wd = weight(1), weight(7)
    diag = add_all([pair_sum[i] for i, _ in FLOW_PAIRS[3:]])
    zeroth = weight(0) * mu[0] + wa * axis_sum + wd * diag

    def first(a):
        axis = 1 + 2 * a
        rest = signed_sum([(VEL[i][a], pair_diff[i]) for i, _ in FLOW_PAIRS[3:] if VEL[i][a]])
        return wa * pair_diff[axis] + wd * rest

    def second(a, b):
        if a == b:
            rest = add_all([pair_sum[i] for i, _ in FLOW_PAIRS[3:] if VEL[i][a]])
            return wa * pair_sum[1 + 2 * a] + wd * rest
        return wd * signed_sum(
            [(VEL[i][a] * VEL[i][b], pair_sum[i]) for i, _ in FLOW_PAIRS[3:] if VEL[i][a] * VEL[i][b]]
        )

    m2 = {(a, b): second(a, b) for a in range(3) for b in range(a, 3)}
    force = []
    for a in range(3):
        bent = add_all([m2[min(a, b), max(a, b)] * v[b] for b in range(3)])
        force.append(3.0 * first(a) + 9.0 * bent - 3.0 * (v[a] * zeroth))
    heat_diff = [mu[i] - mu[j] for i, j in HEAT_PAIRS]
    heat_even = weight(19) * mu[19] + weight(20) * add_all([mu[i] + mu[j] for i, j in HEAT_PAIRS])
    wh = 4.0 * weight(20)
    heat_odd = add_all([heat_diff[a] * (wh * u) for a, u in enumerate((ux, uy, uz))])
    to_heat = INV_TAU * (LIFT * force[2] + heat_even + heat_odd)
    scaled = wh * temper
    pull = [INV_TAU * (force[a] + scaled * heat_diff[a]) for a in range(3)]
    base = INV_TAU * zeroth
    out = [None] * 26
    out[0] = KEEP * mu[0] + base
    for i, j in FLOW_PAIRS:
        proj = signed_sum([(VEL[i][a], pull[a]) for a in range(3) if VEL[i][a]])
        out[i] = KEEP * mu[i] + (base + proj)
        out[j] = KEEP * mu[j] + (base - proj)
    for i in range(19, 26):
        out[i] = KEEP * mu[i] + to_heat
    return out


def merge_kernel(lo, mid, hi, head, tail):
    for n in range(HALO):
        for out, x in ((head, n), (tail, n + HALO)):
            for a in range(6):
                out[n, a, 0:4] = lo[x, a]
                out[n, a, 4:12] = mid[x, a]
                out[n, a, 12:16] = hi[x, a]


def adjoint_planes(k, state_of, bufs, table, region, put):
    first = lane_is(0)
    last = lane_is(DEPTH - 1)

    def one(n):
        at = At(n, HALO - k)
        x = at.by(0)
        fluid = 1.0 - region[0, x]
        fluids = (fluid, jnp.where(last, 0.0, fluid), jnp.where(first, 0.0, fluid))
        state = [state_of(x, a) for a in range(4)]
        for chain, src in enumerate(bufs):
            lam = adjoint_cell(src, table, at, fluids, state[:3], state[3])
            for i in range(26):
                put(chain, n, x, i, lam[i])

    loop(OWN + 2 * k, one)


def backward_kernel(*refs):
    own, gl, gr, slo, shi, elo, emid, ehi, el, er, mom, table, region, names, heat = refs[:15]
    out_a, out_b, slots, la0, la1, lb0, lb1, late, sums, last_a, last_b, sems = refs[15:]

    def gather(x):
        for i in range(26):
            la0[x + HALO, i, 0:4] = slo[i, x]
            la0[x + HALO, i, 4:12] = own[i, x]
            la0[x + HALO, i, 12:16] = shi[i, x]

    loop(OWN, gather)

    def beside(x):
        for i in range(26):
            la0[x, i] = gl[i, x]
            la0[x + HALO + OWN, i] = gr[i, x]

    loop(HALO, beside)

    def settle(x):
        for a in range(6):
            late[x + HALO, a, 0:4] = elo[x, a]
            late[x + HALO, a, 4:12] = emid[x, a]
            late[x + HALO, a, 12:16] = ehi[x, a]

    loop(OWN, settle)

    def flank(x):
        for a in range(6):
            late[x, a] = el[x, a]
            late[x + HALO + OWN, a] = er[x, a]

    loop(HALO, flank)

    def seed(x):
        fluid = 1.0 - region[0, x]
        up = fluid * late[x, 5]
        zero = jnp.zeros_like(up)
        heat = fluid * late[x, 4]
        for i in range(26):
            cz = VEL[i][2]
            lb0[x, i] = heat if i >= 19 else (zero if cz == 0 else (up if cz > 0 else -up))

    loop(WIDE, seed)

    def collect(chain, lam, fresh):
        for n in range(OWN):
            value = lam[n + HALO, RISING][4:12]
            spot = pl.ds(OWN * OWN * chain + OWN * n, OWN)
            sums[spot] = value if fresh else sums[spot] + value

    bufs = [(la0, la1), (lb0, lb1)]
    for k in (3, 2, 1, 0):
        for chain, (src, _) in enumerate(bufs):
            collect(chain, src, k == 3)

        def put(chain, n, x, i, value, k=k, dsts=(bufs[0][1], bufs[1][1])):
            if k == 0:
                (last_a, last_b)[chain][i, n] = value[4:12]
            else:
                dsts[chain][x, i] = value

        def state_of(x, a, k=k):
            return late[x, a] if k == 3 else mom[k, x, a]

        adjoint_planes(k, state_of, [src for src, _ in bufs], table, region, put)
        bufs = [(dst, src) for src, dst in bufs]
    copies = [
        pltpu.make_async_copy(last_a, out_a, sems.at[0]),
        pltpu.make_async_copy(last_b, out_b, sems.at[1]),
    ]
    for copy in copies:
        copy.start()

    line = 0.25 * jnp.transpose(sums[...])[0:1]
    lane = lax.broadcasted_iota(jnp.int32, (1, DEPTH), 1)
    pair = jnp.concatenate([line, jnp.where(lane < OWN * OWN, names[...], heat[...])], 0)
    count = slots.shape[0]

    def spread(n):
        for q in range(8):
            slots[8 * n + q] = pair

    loop(count // 8, spread)
    for copy in copies:
        copy.wait()


def split3(value):
    high = value.astype(jnp.bfloat16)
    rest = value - high.astype(jnp.float32)
    mid = rest.astype(jnp.bfloat16)
    low = (rest - mid.astype(jnp.float32)).astype(jnp.bfloat16)
    return high, mid, low


def tile_kernel(
    scale, told, theta, first, second, part_a, part_b, theta_new, first_new, second_new, nusselt, adjoint, va, vb, sems
):
    copies = [
        pltpu.make_async_copy(part_a, va, sems.at[0]),
        pltpu.make_async_copy(part_b, vb, sems.at[1]),
    ]
    for copy in copies:
        copy.start()
    rows = told.shape[0] // 2
    half = DEPTH // 2
    lane = lax.broadcasted_iota(jnp.int32, (8, DEPTH), 1)
    left = lane < half

    def flux(r, total):
        return total + told[pl.ds(pl.multiple_of(8 * r, 8), 8)]

    total = lax.fori_loop(0, rows // 4, flux, jnp.zeros((8, DEPTH), jnp.float32), unroll=8)
    odd = lax.rem(lax.broadcasted_iota(jnp.int32, (8, DEPTH), 0), 2) == 1
    share = jnp.sum(jnp.where(odd & (lane == half), total, 0.0)) * scale[0]
    nusselt[0, 0] = 1.0 + share

    def one(r, total):
        base = pl.multiple_of(32 * r, 32)
        even_grad = told[pl.ds(base, 8, stride=4)]
        even_name = told[pl.ds(base + 1, 8, stride=4)]
        odd_grad = told[pl.ds(base + 2, 8, stride=4)]
        odd_name = told[pl.ds(base + 3, 8, stride=4)]

        def whole(pair):
            return pair + share * pltpu.roll(pair, half, 1)

        value = jnp.where(left, whole(even_grad), pltpu.roll(whole(odd_grad), half, 1))
        ident = jnp.where(left, even_name, pltpu.roll(odd_name, half, 1)).astype(jnp.int32)
        upper = ident // DEPTH
        lower = ident - upper * DEPTH
        pieces = [piece.astype(jnp.float32) for piece in split3(value)]
        high_is = lax.broadcasted_iota(jnp.int32, (32, DEPTH), 0)
        low_is = lax.broadcasted_iota(jnp.int32, (DEPTH, DEPTH), 0)
        lhs, rhs = [], []
        for q in range(8):
            hot = high_is == jnp.broadcast_to(upper[q : q + 1], (32, DEPTH))
            lhs.append(
                jnp.concatenate(
                    [
                        jnp.where(hot, jnp.broadcast_to(piece[q : q + 1], (32, DEPTH)), 0.0)
                        for piece in pieces
                    ],
                    0,
                ).astype(jnp.bfloat16)
            )
            hot = low_is == jnp.broadcast_to(lower[q : q + 1], (DEPTH, DEPTH))
            rhs.append(jnp.where(hot, 1.0, 0.0).astype(jnp.bfloat16))
        return total + lax.dot_general(
            jnp.concatenate(lhs, 1),
            jnp.concatenate(rhs, 1),
            (((1,), (1,)), ((), ())),
            preferred_element_type=jnp.float32,
        )

    total = lax.fori_loop(0, rows // 16, one, jnp.zeros((96, DEPTH), jnp.float32), unroll=2)
    grad = (total[0:32] + total[32:64]) + total[64:96]
    new_first = BETA_ONE * first[...] + (1.0 - BETA_ONE) * grad
    new_second = BETA_TWO * second[...] + (1.0 - BETA_TWO) * grad * grad
    first_hat = new_first / (1.0 - BETA_ONE**ADAM_STEP)
    second_hat = new_second / (1.0 - BETA_TWO**ADAM_STEP)
    theta_new[...] = theta[...] - LEARN_RATE * first_hat / (jnp.sqrt(second_hat) + ADAM_EPS)
    first_new[...] = new_first
    second_new[...] = new_second
    for copy in copies:
        copy.wait()

    def combine(c):
        adjoint[c] = va[c] + share * vb[c]

    loop(26, combine)


def neighbour(value, axis, step):
    count = lax.axis_size(axis)
    return lax.ppermute(value, axis, [(i, (i + step) % count) for i in range(count)])


def after(value, *earlier):
    return lax.optimization_barrier((value, *earlier))[0]


def window(checkpoint, adjoint_in, solid_mask, tile_map, theta, first_moment, second_moment):
    vmem = pltpu.VMEM
    f32 = jnp.float32
    place = lax.axis_index("st").astype(jnp.int32).reshape(1)
    smem, on_chip = [pltpu.SMEM], pltpu.VMEM
    plane = checkpoint[:, 0]
    tall = vmem((26, 72, DEPTH), f32)
    slots = call(pack_kernel, [(LINES, DEPTH)] * 6, [tall], 12, in_specs=smem + [on_chip])(place, plane)
    packed = dict(zip((0, 2, 3, 4, 5, 6), slots))

    plate = theta[after(tile_map, packed[0])]
    plate = jnp.broadcast_to(plate[:, :, None], (OWN, OWN, DEPTH))
    names = jnp.pad(tile_map.reshape(1, -1).astype(f32), ((0, 0), (0, DEPTH - OWN * OWN)))
    flags, names = lax.optimization_barrier((jnp.stack([solid_mask.astype(f32), plate]), names))
    packed[1], packed[7] = call(
        pack_flags_kernel, [(LINES + FLAG_LINES, DEPTH)] * 2, [tall], 12, in_specs=smem + [on_chip] * 2
    )(place, plane, flags)

    planes = [packed[0]] + [None] * 7
    for k in (5, 3, 1, 7, 2, 6, 4):
        planes[k] = neighbour(packed[k], "st", k)

    def both(value, axis):
        low, high = value
        low = neighbour(low, axis, 1)
        high = neighbour(high, axis, -1)
        return low, high

    halos = []
    lines = 2 * LINES + PLANE_FLAGS
    sent = call(route_first_kernel, [(lines, DEPTH)] * 2, (), 8, in_specs=smem + [on_chip] * 5)(
        place, planes[1], planes[5], planes[3], planes[7], flags
    )
    halos += both(sent, "gx")
    region, table = call(table_kernel, [(2, WIDE, WIDE, DEPTH), (WIDE, 20, WIDE, DEPTH)], mib=8)(
        planes[1], planes[7], flags, *halos
    )
    sent = call(route_second_kernel, [(2 * LINES, DEPTH)] * 2, (), 8, in_specs=smem + [on_chip] * 4)(
        place, planes[0], planes[4], planes[2], planes[6]
    )
    halos += both(sent, "gx")

    slo, shi = both((adjoint_in[:, :, 4:8], adjoint_in[:, :, 0:4]), "st")

    def rows(first):
        part = slice(first, first + HALO)
        return jnp.concatenate([slo[:, part], adjoint_in[:, part], shi[:, part]], 2)

    gl, gr = both((rows(HALO), rows(0)), "gx")

    big = (WIDE, 26, WIDE, DEPTH)
    mom, edge, edge_lo, edge_hi, heat = call(
        forward_kernel,
        [(3, WIDE, 4, WIDE, DEPTH), (OWN, 6, OWN, DEPTH), (OWN, 6, 4, DEPTH), (OWN, 6, 4, DEPTH), (1, DEPTH)],
        [vmem(big, f32), vmem(big, f32), vmem((WIDE, 4, WIDE, DEPTH), f32)],
        12,
        1,
        15,
    )(place, *planes, *halos, table, region)
    elo, ehi = both((edge_hi, edge_lo), "st")
    head, tail = call(merge_kernel, [(HALO, 6, WIDE, DEPTH)] * 2, mib=4)(elo, edge, ehi)
    el, er = both((tail, head), "gx")

    count = lax.axis_size("gx") * lax.axis_size("st")
    mine = (26, OWN, OWN, DEPTH)
    out_a, out_b, slots = call(
        backward_kernel,
        [mine, mine, (count, 2, DEPTH)],
        [vmem(big, f32)] * 4
        + [vmem((WIDE, 6, WIDE, DEPTH), f32), vmem((DEPTH, DEPTH), f32)]
        + [vmem(mine, f32)] * 2
        + [pltpu.SemaphoreType.DMA((2,))],
        24,
        out_specs=[pltpu.HBM, pltpu.HBM, pltpu.VMEM],
    )(adjoint_in, gl, gr, slo, shi, elo, edge, ehi, el, er, mom, table, region, names, heat)
    told = lax.all_to_all(slots, ("gx", "st"), 0, 0, tiled=True)

    scale = jnp.full((1,), 1.0 / (KAPPA * count * OWN * OWN), f32)
    tiles = (theta.shape[0] // DEPTH, DEPTH)
    theta_new, first_new, second_new, nusselt, adjoint = call(
        tile_kernel,
        [tiles] * 3 + [(1, 1), mine],
        [vmem(mine, f32)] * 2 + [pltpu.SemaphoreType.DMA((2,))],
        mib=12,
        in_specs=[pltpu.SMEM] + [pltpu.VMEM] * 4 + [pltpu.HBM] * 2,
        out_specs=[pltpu.VMEM] * 3 + [pltpu.SMEM, pltpu.VMEM],
    )(
        scale,
        told.reshape(2 * count, DEPTH),
        theta.reshape(tiles),
        first_moment.reshape(tiles),
        second_moment.reshape(tiles),
        out_a,
        out_b,
    )
    flat = theta.shape
    return (
        adjoint,
        theta_new.reshape(flat),
        first_new.reshape(flat),
        second_new.reshape(flat),
        nusselt.reshape(()),
    )


def solution(mesh):
    return jax.shard_map(
        window,
        mesh=mesh,
        in_specs=(
            P(None, ("gx", "st"), None, None),
            P(None, "gx", "st", None),
            P("gx", "st", None),
            P("gx", "st"),
            P(),
            P(),
            P(),
        ),
        out_specs=(P(None, "gx", "st", None), P(), P(), P(), P()),
        check_vma=False,
    )
```

```python
import jax
import jax.numpy as jnp
import numpy as np
from jax import lax
from jax.experimental import pallas as pl
from jax.experimental.pallas import tpu as pltpu
from jax.sharding import PartitionSpec as P


ADAM_STEP = 100

VELOCITY = np.array(
    [
        [0, 0, 0],
        [1, 0, 0],
        [-1, 0, 0],
        [0, 1, 0],
        [0, -1, 0],
        [0, 0, 1],
        [0, 0, -1],
        [1, 1, 0],
        [-1, -1, 0],
        [1, -1, 0],
        [-1, 1, 0],
        [1, 0, 1],
        [-1, 0, -1],
        [1, 0, -1],
        [-1, 0, 1],
        [0, 1, 1],
        [0, -1, -1],
        [0, 1, -1],
        [0, -1, 1],
        [0, 0, 0],
        [1, 0, 0],
        [-1, 0, 0],
        [0, 1, 0],
        [0, -1, 0],
        [0, 0, 1],
        [0, 0, -1],
    ],
    dtype=np.int32,
)
VEL = [tuple(int(v) for v in row) for row in VELOCITY]
OPP = [0, 2, 1, 4, 3, 6, 5, 8, 7, 10, 9, 12, 11, 14, 13, 16, 15, 18, 17, 19, 21, 20, 23, 22, 25, 24]
FLOW_PAIRS = [(i, i + 1) for i in range(1, 19, 2)]
HEAT_PAIRS = [(20, 21), (22, 23), (24, 25)]
INV_TAU = 1.25
KEEP = 1.0 - INV_TAU
LIFT = 0.8 * 0.001
MEAN_TEMP = 0.5
KAPPA = 0.075
RISING = 24
LEARN_RATE = 0.05
BETA_ONE = 0.9
BETA_TWO = 0.99
ADAM_EPS = 1e-08

HALO = 4
OWN = 8
WIDE = OWN + 2 * HALO
DEPTH = 128
INTERPRET = False


def weight(i):
    if i < 19:
        return 1.0 / 3.0 if i == 0 else (1.0 / 18.0 if i < 7 else 1.0 / 36.0)
    return 0.25 if i == 19 else 0.125


def call(kernel, outs, scratch=(), mib=8, scalars=0, inputs=None, out_specs=None, in_specs=None):
    extra = {}
    if in_specs:
        extra["in_specs"] = [pl.BlockSpec(memory_space=space) for space in in_specs]
    if scalars:
        extra["in_specs"] = [pl.BlockSpec(memory_space=pltpu.SMEM)] * scalars + [
            pl.BlockSpec(memory_space=pltpu.VMEM)
        ] * (inputs - scalars)
    if out_specs:
        extra["out_specs"] = [pl.BlockSpec(memory_space=space) for space in out_specs]
    return pl.pallas_call(
        kernel,
        out_shape=[jax.ShapeDtypeStruct(s, jnp.float32) for s in outs],
        scratch_shapes=list(scratch),
        compiler_params=pltpu.CompilerParams(vmem_limit_bytes=mib << 20),
        interpret=INTERPRET,
        **extra,
    )


class At:
    def __init__(self, index, offset):
        self.index, self.offset = index, offset

    def by(self, more):
        return self.index + (self.offset + more) if self.offset + more else self.index


def loop(count, fn):
    lax.fori_loop(0, count, lambda i, c: (fn(i), c)[1], 0)


def shifted(value, step_y, step_z):
    if step_y:
        value = pltpu.roll(value, step_y % value.shape[0], 0)
    if step_z:
        value = pltpu.roll(value, step_z % DEPTH, 1)
    return value


def lane_is(k, rows=WIDE):
    return lax.broadcasted_iota(jnp.int32, (rows, DEPTH), 1) == k


def table_of(i):
    if i >= 24:
        return i - 6
    if i >= 19:
        return i - 20
    return i - 1


def add_all(values):
    total = values[0]
    for value in values[1:]:
        total = total + value
    return total


def signed_sum(terms):
    total = None
    for sign, value in terms:
        if total is None:
            total = value if sign > 0 else -value
        else:
            total = total + value if sign > 0 else total - value
    return total


def moments(s):
    diff = {}
    parts = [s[0]]
    for i, j in FLOW_PAIRS:
        parts.append(s[i] + s[j])
        diff[i] = s[i] - s[j]
    density = add_all(parts)
    speed = []
    for axis in range(3):
        speed.append(signed_sum([(VEL[i][axis], diff[i]) for i, _ in FLOW_PAIRS if VEL[i][axis]]))
    temper = add_all([s[i] for i in range(19, 26)])
    return density, speed, temper


def collided(s, density, speed, temper):
    ux, uy, uz = speed
    vz = uz + LIFT * (temper - MEAN_TEMP)
    vel = (ux, uy, vz)
    base = density - 1.5 * (ux * ux + uy * uy + vz * vz)
    out = [None] * 26
    out[0] = KEEP * s[0] + (INV_TAU * weight(0)) * base
    for i, j in FLOW_PAIRS:
        proj = signed_sum([(VEL[i][a], vel[a]) for a in range(3) if VEL[i][a]])
        factor = INV_TAU * weight(i)
        even = factor * base + (4.5 * factor) * (proj * proj)
        odd = (3.0 * factor) * proj
        out[i] = KEEP * s[i] + (even + odd)
        out[j] = KEEP * s[j] + (even - odd)
    out[19] = KEEP * s[19] + (INV_TAU * weight(19)) * temper
    scaled = (INV_TAU * weight(20)) * temper
    for (i, j), u in zip(HEAT_PAIRS, (ux, uy, uz)):
        odd = scaled * (4.0 * u)
        out[i] = KEEP * s[i] + (scaled + odd)
        out[j] = KEEP * s[j] + (scaled - odd)
    return out


LINES = 26 * WIDE
FLAG_LINES = 2 * OWN * 4
PLANE_FLAGS = 2 * HALO * WIDE


def fill_tall(plane, tall):
    def fill(c):
        tall[c, 0:4] = plane[c, 60:64]
        tall[c, 4:68] = plane[c]
        tall[c, 68:72] = plane[c, 0:4]

    loop(26, fill)


def copy_slot(place, tall, k, out):
    base = pl.multiple_of(OWN * lax.rem(place[0] + k, 8), 8)

    def one(c):
        out[pl.ds(pl.multiple_of(WIDE * c, WIDE), WIDE)] = tall[c, pl.ds(base, WIDE)]

    loop(26, one)


def pack_kernel(place, plane, *refs):
    outs, tall = refs[:6], refs[6]
    fill_tall(plane, tall)
    for k, out in zip((0, 2, 3, 4, 5, 6), outs):
        copy_slot(place, tall, k, out)


def pack_flags_kernel(place, plane, flags, up, down, tall):
    fill_tall(plane, tall)
    copy_slot(place, tall, 1, up)
    copy_slot(place, tall, 7, down)
    for f in range(2):
        for x in range(OWN):
            at = LINES + 4 * (OWN * f + x)
            up[at : at + 4] = flags[f, x, 4:8]
            down[at : at + 4] = flags[f, x, 0:4]


def tall_flags(flags, low, high, f, x):
    at = LINES + 4 * (OWN * f + x)
    return ((0, 4, low[at : at + 4]), (4, 12, flags[f, x]), (12, 16, high[at : at + 4]))


def route_kernel(place, pairs, refs, plus, minus):
    for q, k in enumerate(pairs):
        n = lax.rem(place[0] + (8 - k), 8)
        one, two = refs[2 * q], refs[2 * q + 1]

        def move(first, second, q=q):
            def step(c):
                there = pl.ds(pl.multiple_of(32 * c, 32), 32)
                to = pl.ds(pl.multiple_of(32 * c + LINES * q, 32), 32)
                plus[to] = first[there]
                minus[to] = second[there]

            loop(LINES // 32, step)

        @pl.when(n >= HALO)
        def _(move=move, one=one, two=two):
            move(one, two)

        @pl.when(n < HALO)
        def _(move=move, one=one, two=two):
            move(two, one)


FIRST, SECOND = (1, 3), (0, 2)


def route_first_kernel(place, a, b, c, d, flags, plus, minus):
    route_kernel(place, FIRST, (a, b, c, d), plus, minus)
    low, high = a, d
    for f in range(2):
        for n in range(HALO):
            at = 2 * LINES + WIDE * (HALO * f + n)
            for lo, hi, value in tall_flags(flags, low, high, f, n + HALO):
                plus[at + lo : at + hi] = value
            for lo, hi, value in tall_flags(flags, low, high, f, n):
                minus[at + lo : at + hi] = value


def route_second_kernel(place, a, b, c, d, plus, minus):
    route_kernel(place, SECOND, (a, b, c, d), plus, minus)


def table_kernel(low, high, flags, from_left, from_right, region, table):
    for f in range(2):
        for x in range(OWN):
            for lo, hi, value in tall_flags(flags, low, high, f, x):
                region[f, x + HALO, lo:hi] = value
        for n in range(HALO):
            at = 2 * LINES + WIDE * (HALO * f + n)
            region[f, n] = from_left[at : at + WIDE]
            region[f, n + HALO + OWN] = from_right[at : at + WIDE]
    first = lane_is(0)
    last = lane_is(DEPTH - 1)

    def one(n):
        at = At(n, 1)
        x = at.by(0)
        for i in range(1, 19):
            cx, cy, cz = VEL[i]
            value = shifted(region[0, at.by(-cx)], cy, cz)
            if cz:
                edge = first if cz > 0 else last
                if i in (5, 6):
                    table[x, table_of(i + 19)] = jnp.where(edge, -1.0, value)
                value = jnp.where(edge, 1.0, value)
            table[x, table_of(i)] = value

    loop(WIDE - 2, one)


def streamed(p, table, at):
    x = at.by(0)
    s = []
    for i in range(26):
        if i in (0, 19):
            s.append(p[x, i])
            continue
        cx, cy, cz = VEL[i]
        moved = shifted(p[at.by(-cx), i], cy, cz)
        t = table[x, table_of(i)]
        back = p[x, OPP[i]]
        if i >= 24:
            back = t * back
        s.append(jnp.where(t == 0.0, moved, back))
    return s


def forward_kernel(place, *refs):
    planes, halos = refs[:8], refs[8:12]
    table, region, mom, edge, edge_lo, edge_hi, heat, pa, pb, mom3 = refs[12:]
    first = lane_is(0)

    def start(src, x, off=0):
        s = [src[off + WIDE * i : off + WIDE * (i + 1)] for i in range(26)]
        density, speed, temper = moments(s)
        for a, value in enumerate((*speed, temper)):
            mom[0, x, a] = value
        for i, value in enumerate(collided(s, density, speed, temper)):
            pa[x, i] = value

    for k in range(8):
        n = lax.rem(place[0] + (8 - k), 8)
        start(planes[k], n + HALO)
    for group, pairs in enumerate((FIRST, SECOND)):
        for q, k in enumerate(pairs):
            n = lax.rem(place[0] + (8 - k), HALO)
            start(halos[2 * group], n, LINES * q)
            start(halos[2 * group + 1], n + OWN + HALO, LINES * q)

    def arrive(p, at):
        s = streamed(p, table, at)
        s[RISING] = s[RISING] + jnp.where(first, 0.25 * region[1, at.by(0)], 0.0)
        return s

    src, dst = pa, pb
    for k in range(1, 4):

        def one(n, k=k, src=src, dst=dst):
            at = At(n, k)
            x = at.by(0)
            s = arrive(src, at)
            density, speed, temper = moments(s)
            for a, value in enumerate((*speed, temper)):
                if k < 3:
                    mom[k, x, a] = value
                else:
                    mom3[x, a] = value
            for i, value in enumerate(collided(s, density, speed, temper)):
                dst[x, i] = value

        loop(WIDE - 2 * k, one)
        src, dst = dst, src

    def last(n, total):
        at = At(n, HALO)
        x = at.by(0)
        s = arrive(src, at)
        _, speed, temper = moments(s)
        values = [mom3[x, a] for a in range(4)] + [speed[2], temper]
        for a, value in enumerate(values):
            edge[n, a] = value[4:12]
            edge_lo[n, a] = value[4:8]
            edge_hi[n, a] = value[8:12]
        flux = (1.0 - region[0, x]) * speed[2] * temper
        return total + flux[4:12]

    total = lax.fori_loop(0, OWN, last, jnp.zeros((OWN, DEPTH), jnp.float32))
    heat[...] = jnp.broadcast_to(jnp.sum(total), heat.shape)


def adjoint_cell(lam, table, at, fluids, vel, temper):
    x = at.by(0)
    fluid, fluid_up, fluid_down = fluids
    ux, uy, uz = vel
    vz = uz + LIFT * (temper - MEAN_TEMP)
    v = (ux, uy, vz)

    def mu_of(j):
        cx, cy, cz = VEL[j]
        if j in (0, 19):
            return lam[x, j]
        moved = shifted(lam[at.by(cx), j], -cy, -cz)
        keep = fluid if cz == 0 else (fluid_up if cz > 0 else fluid_down)
        return keep * moved + table[x, table_of(OPP[j])] * lam[x, OPP[j]]

    mu = [mu_of(j) for j in range(26)]
    axis_sum = add_all([mu[i] + mu[j] for i, j in FLOW_PAIRS[:3]])
    pair_sum = {i: mu[i] + mu[j] for i, j in FLOW_PAIRS}
    pair_diff = {i: mu[i] - mu[j] for i, j in FLOW_PAIRS}
    wa, wd = weight(1), weight(7)
    diag = add_all([pair_sum[i] for i, _ in FLOW_PAIRS[3:]])
    zeroth = weight(0) * mu[0] + wa * axis_sum + wd * diag

    def first(a):
        axis = 1 + 2 * a
        rest = signed_sum([(VEL[i][a], pair_diff[i]) for i, _ in FLOW_PAIRS[3:] if VEL[i][a]])
        return wa * pair_diff[axis] + wd * rest

    def second(a, b):
        if a == b:
            rest = add_all([pair_sum[i] for i, _ in FLOW_PAIRS[3:] if VEL[i][a]])
            return wa * pair_sum[1 + 2 * a] + wd * rest
        return wd * signed_sum(
            [(VEL[i][a] * VEL[i][b], pair_sum[i]) for i, _ in FLOW_PAIRS[3:] if VEL[i][a] * VEL[i][b]]
        )

    m2 = {(a, b): second(a, b) for a in range(3) for b in range(a, 3)}
    force = []
    for a in range(3):
        bent = add_all([m2[min(a, b), max(a, b)] * v[b] for b in range(3)])
        force.append(3.0 * first(a) + 9.0 * bent - 3.0 * (v[a] * zeroth))
    heat_diff = [mu[i] - mu[j] for i, j in HEAT_PAIRS]
    heat_even = weight(19) * mu[19] + weight(20) * add_all([mu[i] + mu[j] for i, j in HEAT_PAIRS])
    wh = 4.0 * weight(20)
    heat_odd = add_all([heat_diff[a] * (wh * u) for a, u in enumerate((ux, uy, uz))])
    to_heat = INV_TAU * (LIFT * force[2] + heat_even + heat_odd)
    scaled = wh * temper
    pull = [INV_TAU * (force[a] + scaled * heat_diff[a]) for a in range(3)]
    base = INV_TAU * zeroth
    out = [None] * 26
    out[0] = KEEP * mu[0] + base
    for i, j in FLOW_PAIRS:
        proj = signed_sum([(VEL[i][a], pull[a]) for a in range(3) if VEL[i][a]])
        out[i] = KEEP * mu[i] + (base + proj)
        out[j] = KEEP * mu[j] + (base - proj)
    for i in range(19, 26):
        out[i] = KEEP * mu[i] + to_heat
    return out


def merge_kernel(lo, mid, hi, head, tail):
    for n in range(HALO):
        for out, x in ((head, n), (tail, n + HALO)):
            for a in range(6):
                out[n, a, 0:4] = lo[x, a]
                out[n, a, 4:12] = mid[x, a]
                out[n, a, 12:16] = hi[x, a]


def adjoint_planes(k, state_of, bufs, table, region, put):
    first = lane_is(0)
    last = lane_is(DEPTH - 1)

    def one(n):
        at = At(n, HALO - k)
        x = at.by(0)
        fluid = 1.0 - region[0, x]
        fluids = (fluid, jnp.where(last, 0.0, fluid), jnp.where(first, 0.0, fluid))
        state = [state_of(x, a) for a in range(4)]
        for chain, src in enumerate(bufs):
            lam = adjoint_cell(src, table, at, fluids, state[:3], state[3])
            for i in range(26):
                put(chain, n, x, i, lam[i])

    loop(OWN + 2 * k, one)


def backward_kernel(*refs):
    own, gl, gr, slo, shi, elo, emid, ehi, el, er, mom, table, region, names, heat = refs[:15]
    out_a, out_b, slots, la0, la1, lb0, lb1, late, sums, last_a, last_b, sems = refs[15:]

    def gather(x):
        for i in range(26):
            la0[x + HALO, i, 0:4] = slo[i, x]
            la0[x + HALO, i, 4:12] = own[i, x]
            la0[x + HALO, i, 12:16] = shi[i, x]

    loop(OWN, gather)

    def beside(x):
        for i in range(26):
            la0[x, i] = gl[i, x]
            la0[x + HALO + OWN, i] = gr[i, x]

    loop(HALO, beside)

    def settle(x):
        for a in range(6):
            late[x + HALO, a, 0:4] = elo[x, a]
            late[x + HALO, a, 4:12] = emid[x, a]
            late[x + HALO, a, 12:16] = ehi[x, a]

    loop(OWN, settle)

    def flank(x):
        for a in range(6):
            late[x, a] = el[x, a]
            late[x + HALO + OWN, a] = er[x, a]

    loop(HALO, flank)

    def seed(x):
        fluid = 1.0 - region[0, x]
        up = fluid * late[x, 5]
        zero = jnp.zeros_like(up)
        heat = fluid * late[x, 4]
        for i in range(26):
            cz = VEL[i][2]
            lb0[x, i] = heat if i >= 19 else (zero if cz == 0 else (up if cz > 0 else -up))

    loop(WIDE, seed)

    def collect(chain, lam, fresh):
        for n in range(OWN):
            value = lam[n + HALO, RISING][4:12]
            spot = pl.ds(OWN * OWN * chain + OWN * n, OWN)
            sums[spot] = value if fresh else sums[spot] + value

    bufs = [(la0, la1), (lb0, lb1)]
    for k in (3, 2, 1, 0):
        for chain, (src, _) in enumerate(bufs):
            collect(chain, src, k == 3)

        def put(chain, n, x, i, value, k=k, dsts=(bufs[0][1], bufs[1][1])):
            if k == 0:
                (last_a, last_b)[chain][i, n] = value[4:12]
            else:
                dsts[chain][x, i] = value

        def state_of(x, a, k=k):
            return late[x, a] if k == 3 else mom[k, x, a]

        adjoint_planes(k, state_of, [src for src, _ in bufs], table, region, put)
        bufs = [(dst, src) for src, dst in bufs]
    copies = [
        pltpu.make_async_copy(last_a, out_a, sems.at[0]),
        pltpu.make_async_copy(last_b, out_b, sems.at[1]),
    ]
    for copy in copies:
        copy.start()

    line = 0.25 * jnp.transpose(sums[...])[0:1]
    lane = lax.broadcasted_iota(jnp.int32, (1, DEPTH), 1)
    pair = jnp.concatenate([line, jnp.where(lane < OWN * OWN, names[...], heat[...])], 0)
    count = slots.shape[0]

    def spread(n):
        for q in range(8):
            slots[8 * n + q] = pair

    loop(count // 8, spread)
    for copy in copies:
        copy.wait()


def split3(value):
    high = value.astype(jnp.bfloat16)
    rest = value - high.astype(jnp.float32)
    mid = rest.astype(jnp.bfloat16)
    low = (rest - mid.astype(jnp.float32)).astype(jnp.bfloat16)
    return high, mid, low


def tile_kernel(
    scale, told, theta, first, second, part_a, part_b, theta_new, first_new, second_new, nusselt, adjoint, va, vb, sems
):
    copies = [
        pltpu.make_async_copy(part_a, va, sems.at[0]),
        pltpu.make_async_copy(part_b, vb, sems.at[1]),
    ]
    for copy in copies:
        copy.start()
    rows = told.shape[0] // 2
    half = DEPTH // 2
    lane = lax.broadcasted_iota(jnp.int32, (8, DEPTH), 1)
    left = lane < half

    def flux(r, total):
        return total + told[pl.ds(pl.multiple_of(8 * r, 8), 8)]

    total = lax.fori_loop(0, rows // 4, flux, jnp.zeros((8, DEPTH), jnp.float32), unroll=8)
    odd = lax.rem(lax.broadcasted_iota(jnp.int32, (8, DEPTH), 0), 2) == 1
    share = jnp.sum(jnp.where(odd & (lane == half), total, 0.0)) * scale[0]
    nusselt[0, 0] = 1.0 + share

    def one(r, total):
        base = pl.multiple_of(32 * r, 32)
        even_grad = told[pl.ds(base, 8, stride=4)]
        even_name = told[pl.ds(base + 1, 8, stride=4)]
        odd_grad = told[pl.ds(base + 2, 8, stride=4)]
        odd_name = told[pl.ds(base + 3, 8, stride=4)]

        def whole(pair):
            return pair + share * pltpu.roll(pair, half, 1)

        value = jnp.where(left, whole(even_grad), pltpu.roll(whole(odd_grad), half, 1))
        ident = jnp.where(left, even_name, pltpu.roll(odd_name, half, 1)).astype(jnp.int32)
        upper = ident // DEPTH
        lower = ident - upper * DEPTH
        pieces = [piece.astype(jnp.float32) for piece in split3(value)]
        high_is = lax.broadcasted_iota(jnp.int32, (32, DEPTH), 0)
        low_is = lax.broadcasted_iota(jnp.int32, (DEPTH, DEPTH), 0)
        lhs, rhs = [], []
        for q in range(8):
            hot = high_is == jnp.broadcast_to(upper[q : q + 1], (32, DEPTH))
            lhs.append(
                jnp.concatenate(
                    [
                        jnp.where(hot, jnp.broadcast_to(piece[q : q + 1], (32, DEPTH)), 0.0)
                        for piece in pieces
                    ],
                    0,
                ).astype(jnp.bfloat16)
            )
            hot = low_is == jnp.broadcast_to(lower[q : q + 1], (DEPTH, DEPTH))
            rhs.append(jnp.where(hot, 1.0, 0.0).astype(jnp.bfloat16))
        return total + lax.dot_general(
            jnp.concatenate(lhs, 1),
            jnp.concatenate(rhs, 1),
            (((1,), (1,)), ((), ())),
            preferred_element_type=jnp.float32,
        )

    total = lax.fori_loop(0, rows // 16, one, jnp.zeros((96, DEPTH), jnp.float32), unroll=2)
    grad = (total[0:32] + total[32:64]) + total[64:96]
    new_first = BETA_ONE * first[...] + (1.0 - BETA_ONE) * grad
    new_second = BETA_TWO * second[...] + (1.0 - BETA_TWO) * grad * grad
    first_hat = new_first / (1.0 - BETA_ONE**ADAM_STEP)
    second_hat = new_second / (1.0 - BETA_TWO**ADAM_STEP)
    theta_new[...] = theta[...] - LEARN_RATE * first_hat / (jnp.sqrt(second_hat) + ADAM_EPS)
    first_new[...] = new_first
    second_new[...] = new_second
    for copy in copies:
        copy.wait()

    def combine(c):
        adjoint[c] = va[c] + share * vb[c]

    loop(26, combine)


def neighbour(value, axis, step):
    count = lax.axis_size(axis)
    return lax.ppermute(value, axis, [(i, (i + step) % count) for i in range(count)])


def after(value, *earlier):
    return lax.optimization_barrier((value, *earlier))[0]


def window(checkpoint, adjoint_in, solid_mask, tile_map, theta, first_moment, second_moment):
    vmem = pltpu.VMEM
    f32 = jnp.float32
    place = lax.axis_index("st").astype(jnp.int32).reshape(1)
    smem, on_chip = [pltpu.SMEM], pltpu.VMEM
    plane = checkpoint[:, 0]
    tall = vmem((26, 72, DEPTH), f32)
    slots = call(pack_kernel, [(LINES, DEPTH)] * 6, [tall], 12, in_specs=smem + [on_chip])(place, plane)
    packed = dict(zip((0, 2, 3, 4, 5, 6), slots))

    plate = theta[after(tile_map, packed[0])]
    plate = jnp.broadcast_to(plate[:, :, None], (OWN, OWN, DEPTH))
    names = jnp.pad(tile_map.reshape(1, -1).astype(f32), ((0, 0), (0, DEPTH - OWN * OWN)))
    flags, names = lax.optimization_barrier((jnp.stack([solid_mask.astype(f32), plate]), names))
    packed[1], packed[7] = call(
        pack_flags_kernel, [(LINES + FLAG_LINES, DEPTH)] * 2, [tall], 12, in_specs=smem + [on_chip] * 2
    )(place, plane, flags)

    planes = [packed[0]] + [None] * 7
    for k in (2, 6, 4, 5, 3, 1, 7):
        planes[k] = neighbour(packed[k], "st", k)

    def both(value, axis):
        low, high = value
        low = neighbour(low, axis, 1)
        high = neighbour(high, axis, -1)
        return low, high

    sent = call(route_second_kernel, [(2 * LINES, DEPTH)] * 2, (), 8, in_specs=smem + [on_chip] * 4)(
        place, planes[0], planes[4], planes[2], planes[6]
    )
    others = both(sent, "gx")
    lines = 2 * LINES + PLANE_FLAGS
    sent = call(route_first_kernel, [(lines, DEPTH)] * 2, (), 8, in_specs=smem + [on_chip] * 5)(
        place, planes[1], planes[5], planes[3], planes[7], flags
    )
    halos = both(sent, "gx")
    region, table = call(table_kernel, [(2, WIDE, WIDE, DEPTH), (WIDE, 20, WIDE, DEPTH)], mib=8)(
        planes[1], planes[7], flags, *halos
    )
    halos += others

    slo, shi = both((adjoint_in[:, :, 4:8], adjoint_in[:, :, 0:4]), "st")

    def rows(first):
        part = slice(first, first + HALO)
        return jnp.concatenate([slo[:, part], adjoint_in[:, part], shi[:, part]], 2)

    gl, gr = both((rows(HALO), rows(0)), "gx")

    big = (WIDE, 26, WIDE, DEPTH)
    mom, edge, edge_lo, edge_hi, heat = call(
        forward_kernel,
        [(3, WIDE, 4, WIDE, DEPTH), (OWN, 6, OWN, DEPTH), (OWN, 6, 4, DEPTH), (OWN, 6, 4, DEPTH), (1, DEPTH)],
        [vmem(big, f32), vmem(big, f32), vmem((WIDE, 4, WIDE, DEPTH), f32)],
        12,
        1,
        15,
    )(place, *planes, *halos, table, region)
    elo, ehi = both((edge_hi, edge_lo), "st")
    head, tail = call(merge_kernel, [(HALO, 6, WIDE, DEPTH)] * 2, mib=4)(elo, edge, ehi)
    el, er = both((tail, head), "gx")

    count = lax.axis_size("gx") * lax.axis_size("st")
    mine = (26, OWN, OWN, DEPTH)
    out_a, out_b, slots = call(
        backward_kernel,
        [mine, mine, (count, 2, DEPTH)],
        [vmem(big, f32)] * 4
        + [vmem((WIDE, 6, WIDE, DEPTH), f32), vmem((DEPTH, DEPTH), f32)]
        + [vmem(mine, f32)] * 2
        + [pltpu.SemaphoreType.DMA((2,))],
        24,
        out_specs=[pltpu.HBM, pltpu.HBM, pltpu.VMEM],
    )(adjoint_in, gl, gr, slo, shi, elo, edge, ehi, el, er, mom, table, region, names, heat)
    told = lax.all_to_all(slots, ("gx", "st"), 0, 0, tiled=True)

    scale = jnp.full((1,), 1.0 / (KAPPA * count * OWN * OWN), f32)
    tiles = (theta.shape[0] // DEPTH, DEPTH)
    theta_new, first_new, second_new, nusselt, adjoint = call(
        tile_kernel,
        [tiles] * 3 + [(1, 1), mine],
        [vmem(mine, f32)] * 2 + [pltpu.SemaphoreType.DMA((2,))],
        mib=12,
        in_specs=[pltpu.SMEM] + [pltpu.VMEM] * 4 + [pltpu.HBM] * 2,
        out_specs=[pltpu.VMEM] * 3 + [pltpu.SMEM, pltpu.VMEM],
    )(
        scale,
        told.reshape(2 * count, DEPTH),
        theta.reshape(tiles),
        first_moment.reshape(tiles),
        second_moment.reshape(tiles),
        out_a,
        out_b,
    )
    flat = theta.shape
    return (
        adjoint,
        theta_new.reshape(flat),
        first_new.reshape(flat),
        second_new.reshape(flat),
        nusselt.reshape(()),
    )


def solution(mesh):
    return jax.shard_map(
        window,
        mesh=mesh,
        in_specs=(
            P(None, ("gx", "st"), None, None),
            P(None, "gx", "st", None),
            P("gx", "st", None),
            P("gx", "st"),
            P(),
            P(),
            P(),
        ),
        out_specs=(P(None, "gx", "st", None), P(), P(), P(), P()),
        check_vma=False,
    )
```

```python
import jax
import jax.numpy as jnp
import numpy as np
from jax import lax
from jax.experimental import pallas as pl
from jax.experimental.pallas import tpu as pltpu
from jax.sharding import PartitionSpec as P


ADAM_STEP = 100

VELOCITY = np.array(
    [
        [0, 0, 0],
        [1, 0, 0],
        [-1, 0, 0],
        [0, 1, 0],
        [0, -1, 0],
        [0, 0, 1],
        [0, 0, -1],
        [1, 1, 0],
        [-1, -1, 0],
        [1, -1, 0],
        [-1, 1, 0],
        [1, 0, 1],
        [-1, 0, -1],
        [1, 0, -1],
        [-1, 0, 1],
        [0, 1, 1],
        [0, -1, -1],
        [0, 1, -1],
        [0, -1, 1],
        [0, 0, 0],
        [1, 0, 0],
        [-1, 0, 0],
        [0, 1, 0],
        [0, -1, 0],
        [0, 0, 1],
        [0, 0, -1],
    ],
    dtype=np.int32,
)
VEL = [tuple(int(v) for v in row) for row in VELOCITY]
OPP = [0, 2, 1, 4, 3, 6, 5, 8, 7, 10, 9, 12, 11, 14, 13, 16, 15, 18, 17, 19, 21, 20, 23, 22, 25, 24]
FLOW_PAIRS = [(i, i + 1) for i in range(1, 19, 2)]
HEAT_PAIRS = [(20, 21), (22, 23), (24, 25)]
INV_TAU = 1.25
KEEP = 1.0 - INV_TAU
LIFT = 0.8 * 0.001
MEAN_TEMP = 0.5
KAPPA = 0.075
RISING = 24
LEARN_RATE = 0.05
BETA_ONE = 0.9
BETA_TWO = 0.99
ADAM_EPS = 1e-08

HALO = 4
OWN = 8
WIDE = OWN + 2 * HALO
DEPTH = 128
INTERPRET = False


def weight(i):
    if i < 19:
        return 1.0 / 3.0 if i == 0 else (1.0 / 18.0 if i < 7 else 1.0 / 36.0)
    return 0.25 if i == 19 else 0.125


def call(kernel, outs, scratch=(), mib=8, scalars=0, inputs=None, out_specs=None, in_specs=None):
    extra = {}
    if in_specs:
        extra["in_specs"] = [pl.BlockSpec(memory_space=space) for space in in_specs]
    if scalars:
        extra["in_specs"] = [pl.BlockSpec(memory_space=pltpu.SMEM)] * scalars + [
            pl.BlockSpec(memory_space=pltpu.VMEM)
        ] * (inputs - scalars)
    if out_specs:
        extra["out_specs"] = [pl.BlockSpec(memory_space=space) for space in out_specs]
    return pl.pallas_call(
        kernel,
        out_shape=[jax.ShapeDtypeStruct(s, jnp.float32) for s in outs],
        scratch_shapes=list(scratch),
        compiler_params=pltpu.CompilerParams(vmem_limit_bytes=mib << 20),
        interpret=INTERPRET,
        **extra,
    )


class At:
    def __init__(self, index, offset):
        self.index, self.offset = index, offset

    def by(self, more):
        return self.index + (self.offset + more) if self.offset + more else self.index


def loop(count, fn):
    lax.fori_loop(0, count, lambda i, c: (fn(i), c)[1], 0)


def shifted(value, step_y, step_z):
    if step_y:
        value = pltpu.roll(value, step_y % value.shape[0], 0)
    if step_z:
        value = pltpu.roll(value, step_z % DEPTH, 1)
    return value


def lane_is(k, rows=WIDE):
    return lax.broadcasted_iota(jnp.int32, (rows, DEPTH), 1) == k


def table_of(i):
    if i >= 24:
        return i - 6
    if i >= 19:
        return i - 20
    return i - 1


def add_all(values):
    total = values[0]
    for value in values[1:]:
        total = total + value
    return total


def signed_sum(terms):
    total = None
    for sign, value in terms:
        if total is None:
            total = value if sign > 0 else -value
        else:
            total = total + value if sign > 0 else total - value
    return total


def moments(s):
    diff = {}
    parts = [s[0]]
    for i, j in FLOW_PAIRS:
        parts.append(s[i] + s[j])
        diff[i] = s[i] - s[j]
    density = add_all(parts)
    speed = []
    for axis in range(3):
        speed.append(signed_sum([(VEL[i][axis], diff[i]) for i, _ in FLOW_PAIRS if VEL[i][axis]]))
    temper = add_all([s[i] for i in range(19, 26)])
    return density, speed, temper


def collided(s, density, speed, temper):
    ux, uy, uz = speed
    vz = uz + LIFT * (temper - MEAN_TEMP)
    vel = (ux, uy, vz)
    base = density - 1.5 * (ux * ux + uy * uy + vz * vz)
    out = [None] * 26
    out[0] = KEEP * s[0] + (INV_TAU * weight(0)) * base
    for i, j in FLOW_PAIRS:
        proj = signed_sum([(VEL[i][a], vel[a]) for a in range(3) if VEL[i][a]])
        factor = INV_TAU * weight(i)
        even = factor * base + (4.5 * factor) * (proj * proj)
        odd = (3.0 * factor) * proj
        out[i] = KEEP * s[i] + (even + odd)
        out[j] = KEEP * s[j] + (even - odd)
    out[19] = KEEP * s[19] + (INV_TAU * weight(19)) * temper
    scaled = (INV_TAU * weight(20)) * temper
    for (i, j), u in zip(HEAT_PAIRS, (ux, uy, uz)):
        odd = scaled * (4.0 * u)
        out[i] = KEEP * s[i] + (scaled + odd)
        out[j] = KEEP * s[j] + (scaled - odd)
    return out


LINES = 26 * WIDE
FLAG_LINES = 2 * OWN * 4
PLANE_FLAGS = 2 * HALO * WIDE


def fill_tall(plane, tall):
    def fill(c):
        tall[c, 0:4] = plane[c, 60:64]
        tall[c, 4:68] = plane[c]
        tall[c, 68:72] = plane[c, 0:4]

    loop(26, fill)


def copy_slot(place, tall, k, out):
    base = pl.multiple_of(OWN * lax.rem(place[0] + k, 8), 8)

    def one(c):
        out[pl.ds(pl.multiple_of(WIDE * c, WIDE), WIDE)] = tall[c, pl.ds(base, WIDE)]

    loop(26, one)


def pack_kernel(place, plane, *refs):
    outs, tall = refs[:6], refs[6]
    fill_tall(plane, tall)
    for k, out in zip((0, 2, 3, 4, 5, 6), outs):
        copy_slot(place, tall, k, out)


def pack_flags_kernel(place, plane, flags, up, down, tall):
    fill_tall(plane, tall)
    copy_slot(place, tall, 1, up)
    copy_slot(place, tall, 7, down)
    for f in range(2):
        for x in range(OWN):
            at = LINES + 4 * (OWN * f + x)
            up[at : at + 4] = flags[f, x, 4:8]
            down[at : at + 4] = flags[f, x, 0:4]


def tall_flags(flags, low, high, f, x):
    at = LINES + 4 * (OWN * f + x)
    return ((0, 4, low[at : at + 4]), (4, 12, flags[f, x]), (12, 16, high[at : at + 4]))


def route_kernel(place, pairs, refs, plus, minus):
    for q, k in enumerate(pairs):
        n = lax.rem(place[0] + (8 - k), 8)
        one, two = refs[2 * q], refs[2 * q + 1]

        def move(first, second, q=q):
            def step(c):
                there = pl.ds(pl.multiple_of(32 * c, 32), 32)
                to = pl.ds(pl.multiple_of(32 * c + LINES * q, 32), 32)
                plus[to] = first[there]
                minus[to] = second[there]

            loop(LINES // 32, step)

        @pl.when(n >= HALO)
        def _(move=move, one=one, two=two):
            move(one, two)

        @pl.when(n < HALO)
        def _(move=move, one=one, two=two):
            move(two, one)


FIRST, SECOND = (1, 3), (0, 2)


def route_first_kernel(place, a, b, c, d, flags, plus, minus):
    route_kernel(place, FIRST, (a, b, c, d), plus, minus)
    low, high = a, d
    for f in range(2):
        for n in range(HALO):
            at = 2 * LINES + WIDE * (HALO * f + n)
            for lo, hi, value in tall_flags(flags, low, high, f, n + HALO):
                plus[at + lo : at + hi] = value
            for lo, hi, value in tall_flags(flags, low, high, f, n):
                minus[at + lo : at + hi] = value


def route_second_kernel(place, a, b, c, d, plus, minus):
    route_kernel(place, SECOND, (a, b, c, d), plus, minus)


def table_kernel(low, high, flags, from_left, from_right, region, table):
    for f in range(2):
        for x in range(OWN):
            for lo, hi, value in tall_flags(flags, low, high, f, x):
                region[f, x + HALO, lo:hi] = value
        for n in range(HALO):
            at = 2 * LINES + WIDE * (HALO * f + n)
            region[f, n] = from_left[at : at + WIDE]
            region[f, n + HALO + OWN] = from_right[at : at + WIDE]
    first = lane_is(0)
    last = lane_is(DEPTH - 1)

    def one(n):
        at = At(n, 1)
        x = at.by(0)
        for i in range(1, 19):
            cx, cy, cz = VEL[i]
            value = shifted(region[0, at.by(-cx)], cy, cz)
            if cz:
                edge = first if cz > 0 else last
                if i in (5, 6):
                    table[x, table_of(i + 19)] = jnp.where(edge, -1.0, value)
                value = jnp.where(edge, 1.0, value)
            table[x, table_of(i)] = value

    loop(WIDE - 2, one)


def streamed(p, table, at):
    x = at.by(0)
    s = []
    for i in range(26):
        if i in (0, 19):
            s.append(p[x, i])
            continue
        cx, cy, cz = VEL[i]
        moved = shifted(p[at.by(-cx), i], cy, cz)
        t = table[x, table_of(i)]
        back = p[x, OPP[i]]
        if i >= 24:
            back = t * back
        s.append(jnp.where(t == 0.0, moved, back))
    return s


def forward_kernel(place, *refs):
    planes, halos = refs[:8], refs[8:12]
    table, region, mom, edge, edge_lo, edge_hi, heat, pa, pb, mom3 = refs[12:]
    first = lane_is(0)

    def start(src, x, off=0):
        s = [src[off + WIDE * i : off + WIDE * (i + 1)] for i in range(26)]
        density, speed, temper = moments(s)
        for a, value in enumerate((*speed, temper)):
            mom[0, x, a] = value
        for i, value in enumerate(collided(s, density, speed, temper)):
            pa[x, i] = value

    for k in range(8):
        n = lax.rem(place[0] + (8 - k), 8)
        start(planes[k], n + HALO)
    for group, pairs in enumerate((FIRST, SECOND)):
        for q, k in enumerate(pairs):
            n = lax.rem(place[0] + (8 - k), HALO)
            start(halos[2 * group], n, LINES * q)
            start(halos[2 * group + 1], n + OWN + HALO, LINES * q)

    def arrive(p, at):
        s = streamed(p, table, at)
        s[RISING] = s[RISING] + jnp.where(first, 0.25 * region[1, at.by(0)], 0.0)
        return s

    src, dst = pa, pb
    for k in range(1, 4):

        def one(n, k=k, src=src, dst=dst):
            at = At(n, k)
            x = at.by(0)
            s = arrive(src, at)
            density, speed, temper = moments(s)
            for a, value in enumerate((*speed, temper)):
                if k < 3:
                    mom[k, x, a] = value
                else:
                    mom3[x, a] = value
            for i, value in enumerate(collided(s, density, speed, temper)):
                dst[x, i] = value

        loop(WIDE - 2 * k, one)
        src, dst = dst, src

    def last(n, total):
        at = At(n, HALO)
        x = at.by(0)
        s = arrive(src, at)
        _, speed, temper = moments(s)
        values = [mom3[x, a] for a in range(4)] + [speed[2], temper]
        for a, value in enumerate(values):
            edge[n, a] = value[4:12]
            edge_lo[n, a] = value[4:8]
            edge_hi[n, a] = value[8:12]
        flux = (1.0 - region[0, x]) * speed[2] * temper
        return total + flux[4:12]

    total = lax.fori_loop(0, OWN, last, jnp.zeros((OWN, DEPTH), jnp.float32))
    heat[...] = jnp.broadcast_to(jnp.sum(total), heat.shape)


def adjoint_cell(lam, table, at, fluids, vel, temper):
    x = at.by(0)
    fluid, fluid_up, fluid_down = fluids
    ux, uy, uz = vel
    vz = uz + LIFT * (temper - MEAN_TEMP)
    v = (ux, uy, vz)

    def mu_of(j):
        cx, cy, cz = VEL[j]
        if j in (0, 19):
            return lam[x, j]
        moved = shifted(lam[at.by(cx), j], -cy, -cz)
        keep = fluid if cz == 0 else (fluid_up if cz > 0 else fluid_down)
        return keep * moved + table[x, table_of(OPP[j])] * lam[x, OPP[j]]

    mu = [mu_of(j) for j in range(26)]
    axis_sum = add_all([mu[i] + mu[j] for i, j in FLOW_PAIRS[:3]])
    pair_sum = {i: mu[i] + mu[j] for i, j in FLOW_PAIRS}
    pair_diff = {i: mu[i] - mu[j] for i, j in FLOW_PAIRS}
    wa, wd = weight(1), weight(7)
    diag = add_all([pair_sum[i] for i, _ in FLOW_PAIRS[3:]])
    zeroth = weight(0) * mu[0] + wa * axis_sum + wd * diag

    def first(a):
        axis = 1 + 2 * a
        rest = signed_sum([(VEL[i][a], pair_diff[i]) for i, _ in FLOW_PAIRS[3:] if VEL[i][a]])
        return wa * pair_diff[axis] + wd * rest

    def second(a, b):
        if a == b:
            rest = add_all([pair_sum[i] for i, _ in FLOW_PAIRS[3:] if VEL[i][a]])
            return wa * pair_sum[1 + 2 * a] + wd * rest
        return wd * signed_sum(
            [(VEL[i][a] * VEL[i][b], pair_sum[i]) for i, _ in FLOW_PAIRS[3:] if VEL[i][a] * VEL[i][b]]
        )

    m2 = {(a, b): second(a, b) for a in range(3) for b in range(a, 3)}
    force = []
    for a in range(3):
        bent = add_all([m2[min(a, b), max(a, b)] * v[b] for b in range(3)])
        force.append(3.0 * first(a) + 9.0 * bent - 3.0 * (v[a] * zeroth))
    heat_diff = [mu[i] - mu[j] for i, j in HEAT_PAIRS]
    heat_even = weight(19) * mu[19] + weight(20) * add_all([mu[i] + mu[j] for i, j in HEAT_PAIRS])
    wh = 4.0 * weight(20)
    heat_odd = add_all([heat_diff[a] * (wh * u) for a, u in enumerate((ux, uy, uz))])
    to_heat = INV_TAU * (LIFT * force[2] + heat_even + heat_odd)
    scaled = wh * temper
    pull = [INV_TAU * (force[a] + scaled * heat_diff[a]) for a in range(3)]
    base = INV_TAU * zeroth
    out = [None] * 26
    out[0] = KEEP * mu[0] + base
    for i, j in FLOW_PAIRS:
        proj = signed_sum([(VEL[i][a], pull[a]) for a in range(3) if VEL[i][a]])
        out[i] = KEEP * mu[i] + (base + proj)
        out[j] = KEEP * mu[j] + (base - proj)
    for i in range(19, 26):
        out[i] = KEEP * mu[i] + to_heat
    return out


def merge_kernel(lo, mid, hi, head, tail):
    for n in range(HALO):
        for out, x in ((head, n), (tail, n + HALO)):
            for a in range(6):
                out[n, a, 0:4] = lo[x, a]
                out[n, a, 4:12] = mid[x, a]
                out[n, a, 12:16] = hi[x, a]


def adjoint_planes(k, state_of, bufs, table, region, put):
    first = lane_is(0)
    last = lane_is(DEPTH - 1)

    def one(n):
        at = At(n, HALO - k)
        x = at.by(0)
        fluid = 1.0 - region[0, x]
        fluids = (fluid, jnp.where(last, 0.0, fluid), jnp.where(first, 0.0, fluid))
        state = [state_of(x, a) for a in range(4)]
        for chain, src in enumerate(bufs):
            lam = adjoint_cell(src, table, at, fluids, state[:3], state[3])
            for i in range(26):
                put(chain, n, x, i, lam[i])

    loop(OWN + 2 * k, one)


def collect_kernel(own, gl, gr, slo, shi, lam):
    def gather(x):
        for i in range(26):
            lam[x + HALO, i, 0:4] = slo[i, x]
            lam[x + HALO, i, 4:12] = own[i, x]
            lam[x + HALO, i, 12:16] = shi[i, x]

    loop(OWN, gather)

    def beside(x):
        for i in range(26):
            lam[x, i] = gl[i, x]
            lam[x + HALO + OWN, i] = gr[i, x]

    loop(HALO, beside)


def backward_kernel(*refs):
    start, elo, emid, ehi, el, er, mom, table, region, names, heat = refs[:11]
    out_a, out_b, slots, la0, la1, lb0, lb1, late, sums, last_a, last_b, sems = refs[11:]

    def settle(x):
        for a in range(6):
            late[x + HALO, a, 0:4] = elo[x, a]
            late[x + HALO, a, 4:12] = emid[x, a]
            late[x + HALO, a, 12:16] = ehi[x, a]

    loop(OWN, settle)

    def flank(x):
        for a in range(6):
            late[x, a] = el[x, a]
            late[x + HALO + OWN, a] = er[x, a]

    loop(HALO, flank)

    def seed(x):
        fluid = 1.0 - region[0, x]
        up = fluid * late[x, 5]
        zero = jnp.zeros_like(up)
        heat = fluid * late[x, 4]
        for i in range(26):
            cz = VEL[i][2]
            lb0[x, i] = heat if i >= 19 else (zero if cz == 0 else (up if cz > 0 else -up))

    loop(WIDE, seed)

    def collect(chain, lam, fresh):
        for n in range(OWN):
            value = lam[n + HALO, RISING][4:12]
            spot = pl.ds(OWN * OWN * chain + OWN * n, OWN)
            sums[spot] = value if fresh else sums[spot] + value

    bufs = [(start, la1), (lb0, lb1)]
    for k in (3, 2, 1, 0):
        for chain, (src, _) in enumerate(bufs):
            collect(chain, src, k == 3)

        def put(chain, n, x, i, value, k=k, dsts=(bufs[0][1], bufs[1][1])):
            if k == 0:
                (last_a, last_b)[chain][i, n] = value[4:12]
            else:
                dsts[chain][x, i] = value

        def state_of(x, a, k=k):
            return late[x, a] if k == 3 else mom[k, x, a]

        adjoint_planes(k, state_of, [src for src, _ in bufs], table, region, put)
        bufs = [(dst, la0 if src is start else src) for src, dst in bufs]
    copies = [
        pltpu.make_async_copy(last_a, out_a, sems.at[0]),
        pltpu.make_async_copy(last_b, out_b, sems.at[1]),
    ]
    for copy in copies:
        copy.start()

    line = 0.25 * jnp.transpose(sums[...])[0:1]
    lane = lax.broadcasted_iota(jnp.int32, (1, DEPTH), 1)
    pair = jnp.concatenate([line, jnp.where(lane < OWN * OWN, names[...], heat[...])], 0)
    count = slots.shape[0]

    def spread(n):
        for q in range(8):
            slots[8 * n + q] = pair

    loop(count // 8, spread)
    for copy in copies:
        copy.wait()


def split3(value):
    high = value.astype(jnp.bfloat16)
    rest = value - high.astype(jnp.float32)
    mid = rest.astype(jnp.bfloat16)
    low = (rest - mid.astype(jnp.float32)).astype(jnp.bfloat16)
    return high, mid, low


def tile_kernel(
    scale, told, theta, first, second, part_a, part_b, theta_new, first_new, second_new, nusselt, adjoint, va, vb, sems
):
    copies = [
        pltpu.make_async_copy(part_a, va, sems.at[0]),
        pltpu.make_async_copy(part_b, vb, sems.at[1]),
    ]
    for copy in copies:
        copy.start()
    rows = told.shape[0] // 2
    half = DEPTH // 2
    lane = lax.broadcasted_iota(jnp.int32, (8, DEPTH), 1)
    left = lane < half

    def flux(r, total):
        return total + told[pl.ds(pl.multiple_of(8 * r, 8), 8)]

    total = lax.fori_loop(0, rows // 4, flux, jnp.zeros((8, DEPTH), jnp.float32), unroll=8)
    odd = lax.rem(lax.broadcasted_iota(jnp.int32, (8, DEPTH), 0), 2) == 1
    share = jnp.sum(jnp.where(odd & (lane == half), total, 0.0)) * scale[0]
    nusselt[0, 0] = 1.0 + share

    def one(r, total):
        base = pl.multiple_of(32 * r, 32)
        even_grad = told[pl.ds(base, 8, stride=4)]
        even_name = told[pl.ds(base + 1, 8, stride=4)]
        odd_grad = told[pl.ds(base + 2, 8, stride=4)]
        odd_name = told[pl.ds(base + 3, 8, stride=4)]

        def whole(pair):
            return pair + share * pltpu.roll(pair, half, 1)

        value = jnp.where(left, whole(even_grad), pltpu.roll(whole(odd_grad), half, 1))
        ident = jnp.where(left, even_name, pltpu.roll(odd_name, half, 1)).astype(jnp.int32)
        upper = ident // DEPTH
        lower = ident - upper * DEPTH
        pieces = [piece.astype(jnp.float32) for piece in split3(value)]
        high_is = lax.broadcasted_iota(jnp.int32, (32, DEPTH), 0)
        low_is = lax.broadcasted_iota(jnp.int32, (DEPTH, DEPTH), 0)
        lhs, rhs = [], []
        for q in range(8):
            hot = high_is == jnp.broadcast_to(upper[q : q + 1], (32, DEPTH))
            lhs.append(
                jnp.concatenate(
                    [
                        jnp.where(hot, jnp.broadcast_to(piece[q : q + 1], (32, DEPTH)), 0.0)
                        for piece in pieces
                    ],
                    0,
                ).astype(jnp.bfloat16)
            )
            hot = low_is == jnp.broadcast_to(lower[q : q + 1], (DEPTH, DEPTH))
            rhs.append(jnp.where(hot, 1.0, 0.0).astype(jnp.bfloat16))
        return total + lax.dot_general(
            jnp.concatenate(lhs, 1),
            jnp.concatenate(rhs, 1),
            (((1,), (1,)), ((), ())),
            preferred_element_type=jnp.float32,
        )

    total = lax.fori_loop(0, rows // 16, one, jnp.zeros((96, DEPTH), jnp.float32), unroll=2)
    grad = (total[0:32] + total[32:64]) + total[64:96]
    new_first = BETA_ONE * first[...] + (1.0 - BETA_ONE) * grad
    new_second = BETA_TWO * second[...] + (1.0 - BETA_TWO) * grad * grad
    first_hat = new_first / (1.0 - BETA_ONE**ADAM_STEP)
    second_hat = new_second / (1.0 - BETA_TWO**ADAM_STEP)
    theta_new[...] = theta[...] - LEARN_RATE * first_hat / (jnp.sqrt(second_hat) + ADAM_EPS)
    first_new[...] = new_first
    second_new[...] = new_second
    for copy in copies:
        copy.wait()

    def combine(c):
        adjoint[c] = va[c] + share * vb[c]

    loop(26, combine)


def neighbour(value, axis, step):
    count = lax.axis_size(axis)
    return lax.ppermute(value, axis, [(i, (i + step) % count) for i in range(count)])


def after(value, *earlier):
    return lax.optimization_barrier((value, *earlier))[0]


def window(checkpoint, adjoint_in, solid_mask, tile_map, theta, first_moment, second_moment):
    vmem = pltpu.VMEM
    f32 = jnp.float32
    place = lax.axis_index("st").astype(jnp.int32).reshape(1)
    smem, on_chip = [pltpu.SMEM], pltpu.VMEM
    plane = checkpoint[:, 0]
    tall = vmem((26, 72, DEPTH), f32)
    slots = call(pack_kernel, [(LINES, DEPTH)] * 6, [tall], 12, in_specs=smem + [on_chip])(place, plane)
    packed = dict(zip((0, 2, 3, 4, 5, 6), slots))

    plate = theta[after(tile_map, packed[0])]
    plate = jnp.broadcast_to(plate[:, :, None], (OWN, OWN, DEPTH))
    names = jnp.pad(tile_map.reshape(1, -1).astype(f32), ((0, 0), (0, DEPTH - OWN * OWN)))
    flags, names = lax.optimization_barrier((jnp.stack([solid_mask.astype(f32), plate]), names))
    packed[1], packed[7] = call(
        pack_flags_kernel, [(LINES + FLAG_LINES, DEPTH)] * 2, [tall], 12, in_specs=smem + [on_chip] * 2
    )(place, plane, flags)

    planes = [packed[0]] + [None] * 7
    for k in (5, 3, 1, 7, 2, 6, 4):
        planes[k] = neighbour(packed[k], "st", k)

    def both(value, axis):
        low, high = value
        low = neighbour(low, axis, 1)
        high = neighbour(high, axis, -1)
        return low, high

    halos = []
    lines = 2 * LINES + PLANE_FLAGS
    sent = call(route_first_kernel, [(lines, DEPTH)] * 2, (), 8, in_specs=smem + [on_chip] * 5)(
        place, planes[1], planes[5], planes[3], planes[7], flags
    )
    halos += both(sent, "gx")
    region, table = call(table_kernel, [(2, WIDE, WIDE, DEPTH), (WIDE, 20, WIDE, DEPTH)], mib=8)(
        planes[1], planes[7], flags, *halos
    )
    sent = call(route_second_kernel, [(2 * LINES, DEPTH)] * 2, (), 8, in_specs=smem + [on_chip] * 4)(
        place, planes[0], planes[4], planes[2], planes[6]
    )
    halos += both(sent, "gx")

    slo, shi = both((adjoint_in[:, :, 4:8], adjoint_in[:, :, 0:4]), "st")

    def rows(first):
        part = slice(first, first + HALO)
        return jnp.concatenate([slo[:, part], adjoint_in[:, part], shi[:, part]], 2)

    gl, gr = both((rows(HALO), rows(0)), "gx")

    big = (WIDE, 26, WIDE, DEPTH)
    mom, edge, edge_lo, edge_hi, heat = call(
        forward_kernel,
        [(3, WIDE, 4, WIDE, DEPTH), (OWN, 6, OWN, DEPTH), (OWN, 6, 4, DEPTH), (OWN, 6, 4, DEPTH), (1, DEPTH)],
        [vmem(big, f32), vmem(big, f32), vmem((WIDE, 4, WIDE, DEPTH), f32)],
        12,
        1,
        15,
    )(place, *planes, *halos, table, region)
    elo, ehi = both((edge_hi, edge_lo), "st")
    head, tail = call(merge_kernel, [(HALO, 6, WIDE, DEPTH)] * 2, mib=4)(elo, edge, ehi)
    el, er = both((tail, head), "gx")

    lam = call(collect_kernel, [big], mib=4)(adjoint_in, gl, gr, slo, shi)[0]

    count = lax.axis_size("gx") * lax.axis_size("st")
    mine = (26, OWN, OWN, DEPTH)
    out_a, out_b, slots = call(
        backward_kernel,
        [mine, mine, (count, 2, DEPTH)],
        [vmem(big, f32)] * 4
        + [vmem((WIDE, 6, WIDE, DEPTH), f32), vmem((DEPTH, DEPTH), f32)]
        + [vmem(mine, f32)] * 2
        + [pltpu.SemaphoreType.DMA((2,))],
        24,
        out_specs=[pltpu.HBM, pltpu.HBM, pltpu.VMEM],
    )(lam, elo, edge, ehi, el, er, mom, table, region, names, heat)
    told = lax.all_to_all(slots, ("gx", "st"), 0, 0, tiled=True)

    scale = jnp.full((1,), 1.0 / (KAPPA * count * OWN * OWN), f32)
    tiles = (theta.shape[0] // DEPTH, DEPTH)
    theta_new, first_new, second_new, nusselt, adjoint = call(
        tile_kernel,
        [tiles] * 3 + [(1, 1), mine],
        [vmem(mine, f32)] * 2 + [pltpu.SemaphoreType.DMA((2,))],
        mib=12,
        in_specs=[pltpu.SMEM] + [pltpu.VMEM] * 4 + [pltpu.HBM] * 2,
        out_specs=[pltpu.VMEM] * 3 + [pltpu.SMEM, pltpu.VMEM],
    )(
        scale,
        told.reshape(2 * count, DEPTH),
        theta.reshape(tiles),
        first_moment.reshape(tiles),
        second_moment.reshape(tiles),
        out_a,
        out_b,
    )
    flat = theta.shape
    return (
        adjoint,
        theta_new.reshape(flat),
        first_new.reshape(flat),
        second_new.reshape(flat),
        nusselt.reshape(()),
    )


def solution(mesh):
    return jax.shard_map(
        window,
        mesh=mesh,
        in_specs=(
            P(None, ("gx", "st"), None, None),
            P(None, "gx", "st", None),
            P("gx", "st", None),
            P("gx", "st"),
            P(),
            P(),
            P(),
        ),
        out_specs=(P(None, "gx", "st", None), P(), P(), P(), P()),
        check_vma=False,
    )
```
